256 devices in a mesh: row: 16 (over z, core), col: 16 (over y, x).
Axes of the slice: x: 4, y: 4, z: 8, core: 2. Of those that a mesh axis runs over, the one named last changes fastest.
Arguments:
- front_blocks: bfloat16 [64, 5, 512, 512], P('row'), may hold values from -0.125 to 0.125
- block_cols: int32 [64, 5], P('row'), may hold values from 0 to 63, as said below
- samples: bfloat16 [32768, 1024], P('row', 'col'), may hold values from -6 to 6
- sketch_matrix: bfloat16 [1024, 256], replicated, may hold values from -0.1875 to 0.1875
Outputs:
- leaf_bases: bfloat16 [32768, 256], P('row')
- top_transfers: bfloat16 [1024, 256], P('row')
The draws below stay inside these ranges and needn't reach their ends.
Inputs may be any that keep to these rules, and one draw needn't show every extreme that they name: `block_cols`: each row lists 5 different block columns; the first is the row's own index, the second lies in the other half of the 64 block columns (its index differs in the highest bit).
All inputs are finite; a program needn't handle non-finite values.
Results may differ from the reference program's by a relative error of at most 0.035.
Values may be sent and summed in bfloat16 or wider, within the bound.
No kernel may reach another device: no remote copies, remote signals or barrier semaphores. Data moves between devices by JAX's collectives and lax.ppermute only.
A program may use at most 128 MiB of HBM per device.

```python
import math
import jax
import jax.numpy as jnp
from jax import lax

LEAF = 512
RANK = 256
NS = 1024
K = 5
LEAVES = 64
ORDER = 32768
LEVELS = 6


def draw_block_cols(key, part):
    leaf_ids = jnp.arange(LEAVES, dtype=jnp.int32)
    cross_key = jax.random.fold_in(key, 11)
    crossing = LEAVES // 2 + jax.random.randint(cross_key, (LEAVES,), 0, LEAVES // 2, dtype=jnp.int32)
    row_keys = jax.random.split(jax.random.fold_in(key, 12), LEAVES)

    def near_masks(row_key):
        return jax.random.permutation(row_key, LEAVES // 2 - 1)[:K - 2].astype(jnp.int32) + 1
    nearby = jax.vmap(near_masks)(row_keys)
    xor_masks = jnp.concatenate([jnp.zeros((LEAVES, 1), jnp.int32), crossing[:, None], nearby], axis=1)
    return jnp.bitwise_xor(leaf_ids[:, None], xor_masks)


def level_of(rng, shape, shards, low, top_value):
    gain, own = 1.0, jax.random.fold_in(rng, 6)
    for dim, blocks in shards:
        heights = jnp.exp(jax.random.uniform(jax.random.fold_in(own, dim), (blocks,), jnp.float32, low / len(shards), top_value / len(shards)))
        gain = gain * jnp.repeat(heights, shape[dim] // blocks).reshape([-1 if axis == dim else 1 for axis in range(len(shape))])
    return gain


def centred(key, extent, scale, bound, cuts=(), kind=jnp.bfloat16):
    values = scale * jax.random.normal(key, extent, jnp.float32)
    if cuts:
        values = values * level_of(key, extent, cuts, -0.22, 0.18)
    return jnp.clip(values, -bound, bound).astype(kind)


def setup_inputs(seed: int = 0) -> dict:
    seeds = jax.random.split(jax.random.key(seed), 5)
    front_blocks = centred(seeds[0], (LEAVES, K, LEAF, LEAF), (K * LEAF) ** -0.5, 0.125, ((0, 16),))
    block_cols = draw_block_cols(jax.random.fold_in(seeds[4], 71), 0)
    samples = centred(seeds[2], (ORDER, NS), 1.0, 6.0, ((0, 16), (1, 16)))
    sketch_matrix = centred(seeds[3], (NS, RANK), NS ** -0.5, 0.1875)
    return {"front_blocks": front_blocks, "block_cols": block_cols, "samples": samples, "sketch_matrix": sketch_matrix}


def cholqr(sketch):
    highest = lax.Precision.HIGHEST
    gram_matrix = jnp.dot(sketch.T, sketch, precision=highest)
    low_factor = jnp.linalg.cholesky(gram_matrix)
    identity = jnp.eye(sketch.shape[1], dtype=sketch.dtype)
    low_inverse = jax.scipy.linalg.solve_triangular(low_factor, identity, lower=True)
    ortho_basis = jnp.dot(sketch, low_inverse.T, precision=highest)
    return (ortho_basis * math.sqrt(sketch.shape[0])).astype(jnp.bfloat16)

def reference(front_blocks, block_cols, samples, sketch_matrix):
    highest = lax.Precision.HIGHEST
    sketched = jnp.dot(samples.astype(jnp.float32), sketch_matrix.astype(jnp.float32), preferred_element_type=jnp.float32).astype(jnp.bfloat16)
    sample_blocks = sketched.reshape(LEAVES, LEAF, RANK)
    level_ids = jnp.arange(LEVELS, dtype=jnp.int32)

    def one_leaf(inputs):
        blocks, columns, leaf_id = inputs
        gathered_blocks = sample_blocks[columns].astype(jnp.float32)
        products = jnp.einsum('kab,kbc->kac', blocks.astype(jnp.float32), gathered_blocks, precision=highest)
        outside = (jnp.right_shift(leaf_id, level_ids)[:, None] != jnp.right_shift(columns[None, :], level_ids[:, None])).astype(jnp.float32)
        off_samples = jnp.einsum('lk,kac->lac', outside, products, precision=highest).astype(jnp.bfloat16)
        leaf_basis = cholqr(off_samples[0].astype(jnp.float32))
        projected = jnp.einsum('ar,lac->lrc', leaf_basis.astype(jnp.float32), off_samples[1:].astype(jnp.float32), precision=highest)
        projected = (projected * (1.0 / math.sqrt(LEAF))).astype(jnp.bfloat16)
        return (leaf_basis, projected)
    bases, projected = lax.map(one_leaf, (front_blocks, block_cols, jnp.arange(LEAVES, dtype=jnp.int32)))
    transfer = None
    for tree_level in range(1, LEVELS):
        node_count = projected.shape[0] // 2
        paired = projected.reshape(node_count, 2, projected.shape[1], RANK, RANK)
        stacked = jnp.concatenate([paired[:, 0], paired[:, 1]], axis=2)
        transfer = jax.vmap(cholqr)(stacked[:, 0].astype(jnp.float32))
        if tree_level < LEVELS - 1:
            moved = jnp.einsum('npr,nlpc->nlrc', transfer.astype(jnp.float32), stacked[:, 1:].astype(jnp.float32), precision=highest)
            projected = (moved * (1.0 / math.sqrt(2 * RANK))).astype(jnp.bfloat16)
    return (bases.reshape(LEAVES * LEAF, RANK), transfer.reshape(4 * RANK, RANK))
```

```python
import math

import jax
import jax.numpy as jnp
from jax import lax
from jax.experimental import pallas as pl
from jax.experimental.pallas import tpu as pltpu
from jax.sharding import PartitionSpec as P

F32 = jnp.float32
BF16 = jnp.bfloat16
HIGHEST = lax.Precision.HIGHEST


def mm(a, b):
    return lax.dot_general(
        a, b, (((1,), (0,)), ((), ())), precision=HIGHEST, preferred_element_type=F32
    )


def mm_t(a, b):
    return lax.dot_general(
        a, b, (((1,), (1,)), ((), ())), precision=HIGHEST, preferred_element_type=F32
    )


def dot_t(a, b):
    return lax.dot_general(a, b, (((1,), (1,)), ((), ())), preferred_element_type=F32)


def factor64(blocks):
    shape = blocks[0].shape
    sub = lax.broadcasted_iota(jnp.int32, shape, 1)
    rows = list(blocks)
    out = []
    for p in range(8):
        base = 64 + 8 * p
        col = {
            q: [jnp.broadcast_to(rows[q][:, :, base + k : base + k + 1], shape) for k in range(8)]
            for q in range(p, 8)
        }
        a = [[None] * 8 for _ in range(8)]
        for k in range(8):
            for i in range(k, 8):
                a[i][k] = jnp.broadcast_to(col[p][k][:, i : i + 1, :], shape)
        r = [jnp.broadcast_to(rows[p][:, j : j + 1, :], shape) for j in range(8)]
        low = {q: [None] * 8 for q in range(p + 1, 8)}
        joined = None
        for j in range(8):
            pivot = a[j][j]
            inv = 1.0 / pivot
            mult = [None] * 8
            for k in range(j + 1, 8):
                mult[k] = a[k][j] * inv
            for k in range(j + 1, 8):
                for i in range(k, 8):
                    a[i][k] = a[i][k] - mult[k] * a[i][j]
                r[k] = r[k] - mult[k] * r[j]
            for q in range(p + 1, 8):
                low[q][j] = col[q][j] * inv
                for k in range(j + 1, 8):
                    col[q][k] = col[q][k] - mult[k] * col[q][j]
            scaled = r[j] * lax.rsqrt(pivot)
            joined = scaled if joined is None else jnp.where(sub == j, scaled, joined)
        out.append(joined)
        for q in range(p + 1, 8):
            terms = [low[q][j] * r[j] for j in range(8)]
            while len(terms) > 1:
                terms = [terms[i] + terms[i + 1] for i in range(0, len(terms), 2)]
            rows[q] = rows[q] - terms[0]
    return out


def inverse64(wide):
    lane = lax.broadcasted_iota(jnp.int32, (64, 128), 1)
    row = lax.broadcasted_iota(jnp.int32, (64, 128), 0)
    eye = (lane == row).astype(F32)
    full = [jnp.where(lane >= 64, w, eye) for w in wide]
    out = factor64([jnp.stack([f[8 * i : 8 * i + 8] for f in full]) for i in range(8)])
    return [jnp.concatenate([o[b] for o in out], axis=0) for b in range(len(wide))]


def inverse128(blocks):
    n = range(len(blocks))
    lane = lax.broadcasted_iota(jnp.int32, (64, 128), 1)
    row = lax.broadcasted_iota(jnp.int32, (64, 128), 0)
    first = inverse64([pltpu.roll(b[:64], 64, 1) for b in blocks])
    first = [jnp.where(lane < 64, f, 0.0) for f in first]
    right = [mm(first[i][:, :64], blocks[i][:64]) for i in n]
    left = [mm_t(blocks[i][64:, :64], first[i][:, :64]) for i in n]
    schur = [blocks[i][64:] - mm(left[i], right[i]) for i in n]
    mixed = [mm(left[i], first[i]) for i in n]
    second = inverse64(schur)
    eye = (lane == row + 64).astype(F32)
    low = [mm(second[i][:, :64], jnp.where(lane < 64, -mixed[i], eye)) for i in n]
    return [jnp.concatenate([first[i], low[i]], axis=0) for i in n]


def inverse256(grams):
    n = range(len(grams))
    first = inverse128([g[0:128, 0:128] for g in grams])
    right = [mm(first[i], grams[i][0:128, 128:256]) for i in n]
    left = [mm_t(grams[i][128:256, 0:128], first[i]) for i in n]
    schur = [grams[i][128:256, 128:256] - mm(left[i], right[i]) for i in n]
    mixed = [mm(left[i], first[i]) for i in n]
    second = inverse128(schur)
    return [(first[i], -mm(second[i], mixed[i]), second[i]) for i in n]


def cholqr_t(z_ts, gram_ref):
    for i, z_t in enumerate(z_ts):
        gram_ref[i] = dot_t(z_t, z_t)
    inverses = inverse256([gram_ref.at[i] for i in range(len(z_ts))])
    out = []
    for z_t, (top, low, bottom) in zip(z_ts, inverses):
        scale = math.sqrt(z_t.shape[1])
        full = jnp.concatenate(
            [
                jnp.concatenate([top, jnp.zeros_like(top)], axis=1),
                jnp.concatenate([low, bottom], axis=1),
            ],
            axis=0,
        ) * scale
        high = full.astype(BF16)
        rest = (full - high.astype(F32)).astype(BF16)
        out.append(
            jnp.dot(high, z_t, preferred_element_type=F32)
            + jnp.dot(rest, z_t, preferred_element_type=F32)
        )
    return out


VMEM = pl.BlockSpec(memory_space=pltpu.MemorySpace.VMEM)
SMEM = pl.BlockSpec(memory_space=pltpu.MemorySpace.SMEM)
PARAMS = pltpu.CompilerParams(vmem_limit_bytes=48 << 20)


def sketch_kernel(x_ref, w_ref, out_ref):
    sources, rows, depth = x_ref.shape
    rank = w_ref.shape[1]
    total = None
    for s in range(sources):
        part = lax.dot_general(
            w_ref[s * depth : (s + 1) * depth, :], x_ref[s],
            (((0,), (1,)), ((), ())), preferred_element_type=F32,
        )
        total = part if total is None else total + part
    pieces = total.astype(BF16).reshape(sources, rank // sources, rows)
    for r in range(out_ref.shape[0]):
        out_ref[r] = pieces


def sketch(x, w, size_rows):
    sources, rows, _ = x.shape
    shape = (size_rows, sources, w.shape[1] // sources, rows)
    return pl.pallas_call(
        sketch_kernel,
        out_shape=jax.ShapeDtypeStruct(shape, BF16),
        in_specs=[VMEM, VMEM],
        out_specs=VMEM,
        compiler_params=PARAMS,
    )(x, w)


def products_kernel(slot_ref, block_ref, front_ref, sk_ref, out_ref, acc_ref):
    leaf, step = pl.program_id(0), pl.program_id(1)
    block = block_ref[leaf, step]
    pieces = front_ref.shape[3] // sk_ref.shape[3]
    sk = jnp.concatenate([sk_ref[block, q] for q in range(pieces)], axis=1)
    part = dot_t(sk, front_ref[0, 0])

    @pl.when(step == 0)
    def _():
        acc_ref[...] = part

    @pl.when(step > 0)
    def _():
        acc_ref[...] += part

    out_ref[0, 0] = acc_ref[...].astype(BF16)


def products(slots, blocks, front, sk):
    leaves, _, size, _ = front.shape
    steps = slots.shape[1]
    cols = sk.shape[2]
    return pl.pallas_call(
        products_kernel,
        out_shape=jax.ShapeDtypeStruct((steps, leaves, cols, size), BF16),
        grid_spec=pltpu.PrefetchScalarGridSpec(
            num_scalar_prefetch=2,
            grid=(leaves, steps),
            in_specs=[
                pl.BlockSpec((1, 1, size, size), lambda m, s, slot, block: (m, slot[m, s], 0, 0)),
                pl.BlockSpec(sk.shape, lambda m, s, slot, block: (0, 0, 0, 0)),
            ],
            out_specs=pl.BlockSpec(
                (1, 1, cols, size), lambda m, s, slot, block: (steps - 1 - s, m, 0, 0)
            ),
            scratch_shapes=[pltpu.VMEM((cols, size), F32)],
        ),
        compiler_params=PARAMS,
    )(slots, blocks, front, sk)


def leaf_kernel(z_ref, basis_ref, basis_t_ref, gram_ref):
    leaves, size = z_ref.shape[1], z_ref.shape[3]
    rank = z_ref.shape[0] * z_ref.shape[2]
    z_ts = [z_ref[:, m].reshape(rank, size) for m in range(leaves)]
    for m, q_t in enumerate(cholqr_t(z_ts, gram_ref)):
        basis_t_ref[m] = q_t.astype(BF16)
        basis_ref[m] = q_t.T.astype(BF16)


def leaf_bases(z):
    sources, leaves, cols, size = z.shape
    rank = sources * cols
    return pl.pallas_call(
        leaf_kernel,
        out_shape=(
            jax.ShapeDtypeStruct((leaves, size, rank), BF16),
            jax.ShapeDtypeStruct((leaves, rank, size), BF16),
        ),
        in_specs=[VMEM],
        out_specs=(VMEM, VMEM),
        scratch_shapes=[pltpu.VMEM((leaves, rank, rank), F32)],
        compiler_params=PARAMS,
    )(z)


def move(stacked, transfer, scale):
    return (dot_t(stacked, transfer) * scale).astype(BF16)


def local_levels_kernel(pick_ref, z_ref, rest_ref, basis_t_ref, out_ref, proj_ref, next_ref, gram_ref):
    leaves, size = z_ref.shape[1], z_ref.shape[3]
    rank = z_ref.shape[0] * z_ref.shape[2]
    levels = pick_ref.shape[1]
    scale = 1.0 / math.sqrt(size)
    for m in range(leaves):
        basis_t = basis_t_ref[m]
        proj_ref[0, m] = move(z_ref[:, m].reshape(rank, size), basis_t, scale)
        for d in range(rest_ref.shape[1]):
            proj_ref[d + 1, m] = move(rest_ref[:, d, m].reshape(rank, size), basis_t, scale)

    def stack1(level, p):
        return jnp.concatenate(
            [proj_ref[pick_ref[m, level - 1], m] for m in (2 * p, 2 * p + 1)], axis=1
        )

    scale = 1.0 / math.sqrt(2 * rank)
    for p, e_t in enumerate(cholqr_t([stack1(1, p) for p in range(leaves // 2)], gram_ref)):
        e_t = e_t.astype(BF16)
        for level in range(2, levels + 1):
            next_ref[level - 2, p] = move(stack1(level, p), e_t, scale)

    def stack2(level):
        return jnp.concatenate([next_ref[level - 2, 0], next_ref[level - 2, 1]], axis=1)

    e_t = cholqr_t([stack2(2)], gram_ref)[0].astype(BF16)
    for level in range(3, levels + 1):
        out_ref[level - 3] = move(stack2(level), e_t, scale)


def local_levels(pick, z, rest, basis_t):
    leaves, rank, _ = basis_t.shape
    levels = pick.shape[1]
    return pl.pallas_call(
        local_levels_kernel,
        out_shape=jax.ShapeDtypeStruct((levels - 2, rank, rank), BF16),
        in_specs=[SMEM, VMEM, VMEM, VMEM],
        out_specs=VMEM,
        scratch_shapes=[
            pltpu.VMEM((rest.shape[1] + 1, leaves, rank, rank), BF16),
            pltpu.VMEM((levels - 1, leaves // 2, rank, rank), BF16),
            pltpu.VMEM((leaves // 2, rank, rank), F32),
        ],
        compiler_params=PARAMS,
    )(pick, z, rest, basis_t)


def pair_t(side_ref, own, partner):
    is_left = side_ref[0] == 0
    left = jnp.where(is_left, own, partner)
    right = jnp.where(is_left, partner, own)
    return jnp.concatenate([left, right], axis=1)


def pair_level_kernel(side_ref, own_ref, partner_ref, out_ref, gram_ref):
    levels, rank, _ = own_ref.shape
    scale = 1.0 / math.sqrt(2 * rank)
    e_t = cholqr_t([pair_t(side_ref, own_ref[0], partner_ref[0])], gram_ref)[0].astype(BF16)
    for level in range(1, levels):
        out_ref[level - 1] = move(pair_t(side_ref, own_ref[level], partner_ref[level]), e_t, scale)


def pair_level(side, own, partner):
    levels, rank, _ = own.shape
    return pl.pallas_call(
        pair_level_kernel,
        out_shape=jax.ShapeDtypeStruct((levels - 1, rank, rank), BF16),
        in_specs=[SMEM, VMEM, VMEM],
        out_specs=VMEM,
        scratch_shapes=[pltpu.VMEM((1, rank, rank), F32)],
        compiler_params=PARAMS,
    )(side, own, partner)


def top_level_kernel(side_ref, own_ref, partner_ref, out_ref, gram_ref, full_ref):
    rows = out_ref.shape[0]
    e_t = cholqr_t([pair_t(side_ref, own_ref[0], partner_ref[0])], gram_ref)[0]
    full_ref[...] = e_t.T
    start = pl.multiple_of(side_ref[1] * rows, rows)
    out_ref[...] = full_ref[pl.ds(start, rows), :].astype(BF16)


def top_level(side, own, partner, rows):
    rank = own.shape[1]
    return pl.pallas_call(
        top_level_kernel,
        out_shape=jax.ShapeDtypeStruct((rows, rank), BF16),
        in_specs=[SMEM, VMEM, VMEM],
        out_specs=VMEM,
        scratch_shapes=[pltpu.VMEM((1, rank, rank), F32), pltpu.VMEM((2 * rank, rank), F32)],
        compiler_params=PARAMS,
    )(side, own, partner)


def plan(block_cols, leaf_ids, top_level):
    level_ids = jnp.arange(top_level, dtype=jnp.int32)
    near = block_cols[:, 2:]
    outside = (
        jnp.right_shift(leaf_ids[:, None, None], level_ids)
        != jnp.right_shift(near[:, :, None], level_ids)
    )
    drop = jnp.sum(outside.astype(jnp.int32), axis=2)
    count = near.shape[1]
    slot_ids = jnp.arange(count, dtype=jnp.int32)
    before = (drop[:, None, :] > drop[:, :, None]) | (
        (drop[:, None, :] == drop[:, :, None]) & (slot_ids[None, None, :] < slot_ids[None, :, None])
    )
    rank = jnp.sum(before.astype(jnp.int32), axis=2)
    chosen = (rank[:, None, :] == slot_ids[None, :, None]).astype(jnp.int32)
    one = jnp.ones_like(near[:, :1])
    slots = jnp.concatenate([one, jnp.sum(chosen * (slot_ids + 2), axis=2)], axis=1)
    blocks = jnp.concatenate([block_cols[:, 1:2], jnp.sum(chosen * near[:, None, :], axis=2)], axis=1)
    pick = jnp.sum((drop[:, None, :] <= level_ids[None, 1:, None]).astype(jnp.int32), axis=2)
    return slots, blocks, pick


def shards(front_blocks, block_cols, samples, sketch_matrix):
    leaf_dev, _, leaf_size, _ = front_blocks.shape
    rank_size = sketch_matrix.shape[1]
    size_rows, size_cols = lax.axis_size("row"), lax.axis_size("col")
    row_index = lax.axis_index("row")
    top = (leaf_dev * size_rows).bit_length() - 1
    leaf_ids = row_index * leaf_dev + jnp.arange(leaf_dev, dtype=jnp.int32)
    slots, blocks, pick = plan(block_cols, leaf_ids, top)

    chunk = samples.shape[0] // size_cols
    mine = lax.all_to_all(samples.reshape(size_cols, chunk, samples.shape[1]), "col", 0, 0)
    pieces = sketch(mine, sketch_matrix, size_rows)
    pieces = pieces.reshape((size_rows * size_cols,) + pieces.shape[2:])
    sk = lax.all_to_all(pieces, ("row", "col"), 0, 0)
    sk = sk.reshape(leaf_dev * size_rows, leaf_size // chunk, sk.shape[1], chunk)

    sums = products(slots, blocks, front_blocks, sk)
    first = jnp.broadcast_to(sums[:1], (size_cols,) + sums.shape[1:])
    rest = lax.all_gather(sums[1:], "col")
    z = lax.all_to_all(first, "col", 0, 0)
    basis, basis_t = leaf_bases(z)
    carried = local_levels(pick, z, rest, basis_t)

    bit = 0
    out_rows = 4 * rank_size // size_rows
    while True:
        partner = lax.ppermute(
            carried, "row", [(s, s ^ (1 << bit)) for s in range(size_rows)]
        )
        side = jnp.stack(
            [jnp.right_shift(row_index, bit) & 1, row_index % (size_rows // 2)]
        ).astype(jnp.int32)
        if carried.shape[0] == 1:
            break
        carried = pair_level(side, carried, partner)
        bit += 1
    top_rows = top_level(side, carried, partner, out_rows)
    return basis.reshape(leaf_dev * leaf_size, rank_size), top_rows


def solution(mesh):
    placed = (P("row", None, None, None), P("row", None), P("row", "col"), P())
    return jax.shard_map(
        shards,
        mesh=mesh,
        in_specs=placed,
        out_specs=(P("row", None), P("row", None)),
        check_vma=False,
    )
```

```python
import math

import jax
import jax.numpy as jnp
from jax import lax
from jax.experimental import pallas as pl
from jax.experimental.pallas import tpu as pltpu
from jax.sharding import PartitionSpec as P

F32 = jnp.float32
BF16 = jnp.bfloat16


NN = (((1,), (0,)), ((), ()))
NT = (((1,), (1,)), ((), ()))


def split(x):
    high = x.astype(BF16)
    return high, (x - high.astype(F32)).astype(BF16)


def product(a, b, dims):
    a_high, a_low = split(a)
    b_high, b_low = split(b)

    def dot(x, y):
        return lax.dot_general(x, y, dims, preferred_element_type=F32)

    return dot(a_high, b_high) + (dot(a_high, b_low) + dot(a_low, b_high))


def mm(a, b):
    return product(a, b, NN)


def mm_t(a, b):
    return product(a, b, NT)


def dot_t(a, b):
    return lax.dot_general(a, b, (((1,), (1,)), ((), ())), preferred_element_type=F32)


def factor64(blocks, width, paired, far):
    shape = blocks[0].shape
    sub = lax.broadcasted_iota(jnp.int32, shape, 1)
    rows = list(blocks)
    out = [None] * 8
    for start in range(0, 64, width):
        own = start // 8
        below = list(range((start + width) // 8, 8))

        def spread(q):
            return [
                jnp.broadcast_to(rows[q][:, :, 64 + start + k : 65 + start + k], shape)
                for k in range(width)
            ]

        mine = spread(own)
        col = {q: list(mine) if q == own else spread(q) for q in below}
        late = [q for q in below if far and q > own + 1]
        near = [q for q in below if q not in late]
        a = [[None] * width for _ in range(width)]
        r = []
        for k in range(width):
            at = (start + k) % 8
            r.append(jnp.broadcast_to(rows[own][:, at : at + 1, :], shape))
            for i in range(k, width):
                at = (start + i) % 8
                a[i][k] = jnp.broadcast_to(mine[k][:, at : at + 1, :], shape)
        low = {q: [None] * width for q in near}
        mult = [[None] * width for _ in range(width)]
        inv = [None] * width
        scaled = [None] * width
        if paired:
            for j in range(0, width, 2):
                p, s, t = a[j][j], a[j + 1][j], a[j + 1][j + 1]
                root = lax.rsqrt(p * t - s * s)
                inv_det = root * root
                p_inv, s_inv, t_inv = t * inv_det, -(s * inv_det), p * inv_det
                m, n = {}, {}
                for k in range(j + 2, width):
                    m[k] = (t * a[k][j] - s * a[k][j + 1]) * inv_det
                    n[k] = (p * a[k][j + 1] - s * a[k][j]) * inv_det
                for k in range(j + 2, width):
                    for i in range(k, width):
                        a[i][k] = a[i][k] - (m[k] * a[i][j] + n[k] * a[i][j + 1])
                    r[k] = r[k] - (m[k] * r[j] + n[k] * r[j + 1])
                for q in near:
                    c, d = col[q][j], col[q][j + 1]
                    low[q][j] = c * p_inv + d * s_inv
                    low[q][j + 1] = c * s_inv + d * t_inv
                    for k in range(j + 2, width):
                        col[q][k] = col[q][k] - (m[k] * c + n[k] * d)
                first = lax.rsqrt(p)
                scaled[j] = r[j] * first
                scaled[j + 1] = (r[j + 1] - (s * (first * first)) * r[j]) * ((p * first) * root)
        else:
            for j in range(width):
                root = lax.rsqrt(a[j][j])
                inv[j] = root * root
                for k in range(j + 1, width):
                    mult[j][k] = a[k][j] * inv[j]
                for k in range(j + 1, width):
                    for i in range(k, width):
                        a[i][k] = a[i][k] - mult[j][k] * a[i][j]
                    r[k] = r[k] - mult[j][k] * r[j]
                for q in near:
                    low[q][j] = col[q][j] * inv[j]
                    for k in range(j + 1, width):
                        col[q][k] = col[q][k] - mult[j][k] * col[q][j]
                scaled[j] = r[j] * root
        for j in range(width):
            at = (start + j) % 8
            out[own] = scaled[j] if at == 0 else jnp.where(sub == at, scaled[j], out[own])
        solved = [None] * width
        if late:
            for j in reversed(range(width)):
                value = r[j] * inv[j]
                for k in range(j + 1, width):
                    value = value - mult[j][k] * solved[k]
                solved[j] = value
        for q in below:
            if q in late:
                terms = [col[q][j] * solved[j] for j in range(width)]
            else:
                terms = [low[q][j] * r[j] for j in range(width)]
            while len(terms) > 1:
                terms = [terms[i] + terms[i + 1] for i in range(0, len(terms), 2)]
            rows[q] = rows[q] - terms[0]
    return out


FORMS = {1: (8, True, False), 2: (8, False, False), 4: (4, False, True)}


def inverse64(wide):
    lane = lax.broadcasted_iota(jnp.int32, (64, 128), 1)
    row = lax.broadcasted_iota(jnp.int32, (64, 128), 0)
    eye = (lane == row).astype(F32)
    full = [jnp.where(lane >= 64, w, eye) for w in wide]
    form = FORMS.get(len(wide), (4, False, True))
    out = factor64([jnp.stack([f[8 * i : 8 * i + 8] for f in full]) for i in range(8)], *form)
    return [jnp.concatenate([o[b] for o in out], axis=0) for b in range(len(wide))]


def inverse128(blocks):
    n = range(len(blocks))
    lane = lax.broadcasted_iota(jnp.int32, (64, 128), 1)
    row = lax.broadcasted_iota(jnp.int32, (64, 128), 0)
    first = inverse64([pltpu.roll(b[:64], 64, 1) for b in blocks])
    first = [jnp.where(lane < 64, f, 0.0) for f in first]
    right = [mm(first[i][:, :64], blocks[i][:64]) for i in n]
    left = [mm_t(blocks[i][64:, :64], first[i][:, :64]) for i in n]
    schur = [blocks[i][64:] - mm(left[i], right[i]) for i in n]
    mixed = [mm(left[i], first[i]) for i in n]
    second = inverse64(schur)
    eye = (lane == row + 64).astype(F32)
    low = [mm(second[i][:, :64], jnp.where(lane < 64, -mixed[i], eye)) for i in n]
    return [jnp.concatenate([first[i], low[i]], axis=0) for i in n]


def cholqr_t(z_ts, gram_ref):
    n = range(len(z_ts))
    half = z_ts[0].shape[0] // 2
    for i in n:
        gram_ref[i] = dot_t(z_ts[i], z_ts[i])
    first = inverse128([gram_ref[i, 0:half, 0:half] for i in n])
    right = [mm(first[i], gram_ref[i, 0:half, half:]) for i in n]
    left = [mm_t(gram_ref[i, half:, 0:half], first[i]) for i in n]
    schur = [gram_ref[i, half:, half:] - mm(left[i], right[i]) for i in n]
    top = []
    for i in n:
        high, low = split(first[i])
        z_1 = z_ts[i][:half]
        top.append(
            jnp.dot(high, z_1, preferred_element_type=F32)
            + jnp.dot(low, z_1, preferred_element_type=F32)
        )
    below = [z_ts[i][half:].astype(F32) - mm(left[i], top[i]) for i in n]
    second = inverse128(schur)
    scale = math.sqrt(z_ts[0].shape[1])
    return [jnp.concatenate([top[i], mm(second[i], below[i])], axis=0) * scale for i in n]


VMEM = pl.BlockSpec(memory_space=pltpu.MemorySpace.VMEM)
SMEM = pl.BlockSpec(memory_space=pltpu.MemorySpace.SMEM)
PARAMS = pltpu.CompilerParams(vmem_limit_bytes=48 << 20)


def partial_kernel(col_ref, x_t_ref, w_ref, out_ref):
    depth = x_t_ref.shape[0]
    start = pl.multiple_of(col_ref[0] * depth, depth)
    part = lax.dot_general(
        w_ref[pl.ds(start, depth), :], x_t_ref[...],
        (((0,), (0,)), ((), ())), preferred_element_type=F32,
    )
    out_ref[...] = part.astype(BF16).reshape(out_ref.shape)


def partial_sketch(col, x_t, w, size_cols):
    shape = (size_cols, w.shape[1] // size_cols, x_t.shape[1])
    return pl.pallas_call(
        partial_kernel,
        out_shape=jax.ShapeDtypeStruct(shape, BF16),
        in_specs=[SMEM, VMEM, VMEM],
        out_specs=VMEM,
        compiler_params=PARAMS,
    )(col, x_t, w)


def sum_kernel(parts_ref, out_ref):
    leaves, _, size = out_ref.shape
    for m in range(leaves):
        at = slice(m * size, (m + 1) * size)
        total = parts_ref[0, :, at].astype(F32)
        for s in range(1, parts_ref.shape[0]):
            total = total + parts_ref[s, :, at].astype(F32)
        out_ref[m] = total.astype(BF16)


def sum_parts(parts, leaves):
    _, cols, rows = parts.shape
    return pl.pallas_call(
        sum_kernel,
        out_shape=jax.ShapeDtypeStruct((leaves, cols, rows // leaves), BF16),
        in_specs=[VMEM],
        out_specs=VMEM,
        compiler_params=PARAMS,
    )(parts)


def products_kernel(slot_ref, block_ref, other_ref, front_ref, mine_ref, theirs_ref, first_ref, rest_ref):
    leaves, steps = slot_ref.shape
    cols = mine_ref.shape[1]
    for m in range(leaves):
        total = None
        for s in range(steps):
            block = block_ref[m, s]
            sk = jnp.where(other_ref[m, s] == 0, mine_ref[block], theirs_ref[block])
            wide = jnp.concatenate([sk] * (steps - s) + [jnp.zeros_like(sk)] * s, axis=0)
            part = dot_t(front_ref[m, slot_ref[m, s]], wide)
            total = part if total is None else total + part
        sums = total.T.astype(BF16)
        for d in range(first_ref.shape[0]):
            first_ref[d, m] = sums[:cols]
        for d in range(1, steps):
            rest_ref[d - 1, m] = sums[d * cols : (d + 1) * cols]


def products(slots, blocks, others, front, mine, theirs, copies):
    leaves, _, size, _ = front.shape
    steps = slots.shape[1]
    cols = mine.shape[1]
    return pl.pallas_call(
        products_kernel,
        out_shape=(
            jax.ShapeDtypeStruct((copies, leaves, cols, size), BF16),
            jax.ShapeDtypeStruct((steps - 1, leaves, cols, size), BF16),
        ),
        in_specs=[SMEM, SMEM, SMEM, VMEM, VMEM, VMEM],
        out_specs=(VMEM, VMEM),
        compiler_params=PARAMS,
    )(slots, blocks, others, front, mine, theirs)


def leaf_kernel(z_ref, basis_ref, basis_t_ref, gram_ref):
    leaves, size = z_ref.shape[1], z_ref.shape[3]
    rank = z_ref.shape[0] * z_ref.shape[2]
    z_ts = [z_ref[:, m].reshape(rank, size) for m in range(leaves)]
    for m, q_t in enumerate(cholqr_t(z_ts, gram_ref)):
        basis_t_ref[m] = q_t.astype(BF16)
        basis_ref[m] = q_t.T.astype(BF16)


def leaf_bases(z):
    sources, leaves, cols, size = z.shape
    rank = sources * cols
    return pl.pallas_call(
        leaf_kernel,
        out_shape=(
            jax.ShapeDtypeStruct((leaves, size, rank), BF16),
            jax.ShapeDtypeStruct((leaves, rank, size), BF16),
        ),
        in_specs=[VMEM],
        out_specs=(VMEM, VMEM),
        scratch_shapes=[pltpu.VMEM((leaves, rank, rank), F32)],
        compiler_params=PARAMS,
    )(z)


def move(stacked, transfer, scale):
    return (dot_t(stacked, transfer) * scale).astype(BF16)


def local_levels_kernel(pick_ref, z_ref, rest_ref, basis_t_ref, out_ref, proj_ref, next_ref, gram_ref):
    leaves, size = z_ref.shape[1], z_ref.shape[3]
    rank = z_ref.shape[0] * z_ref.shape[2]
    levels = pick_ref.shape[1]
    scale = 1.0 / math.sqrt(size)
    for m in range(leaves):
        basis_t = basis_t_ref[m]
        proj_ref[0, m] = move(z_ref[:, m].reshape(rank, size), basis_t, scale)
        for d in range(rest_ref.shape[1]):
            proj_ref[d + 1, m] = move(rest_ref[:, d, m].reshape(rank, size), basis_t, scale)

    def stack1(level, p):
        return jnp.concatenate(
            [proj_ref[pick_ref[m, level - 1], m] for m in (2 * p, 2 * p + 1)], axis=1
        )

    scale = 1.0 / math.sqrt(2 * rank)
    for p, e_t in enumerate(cholqr_t([stack1(1, p) for p in range(leaves // 2)], gram_ref)):
        e_t = e_t.astype(BF16)
        for level in range(2, levels + 1):
            next_ref[level - 2, p] = move(stack1(level, p), e_t, scale)

    def stack2(level):
        return jnp.concatenate([next_ref[level - 2, 0], next_ref[level - 2, 1]], axis=1)

    e_t = cholqr_t([stack2(2)], gram_ref)[0].astype(BF16)
    for level in range(3, levels + 1):
        out_ref[level - 3] = move(stack2(level), e_t, scale)


def local_levels(pick, z, rest, basis_t):
    leaves, rank, _ = basis_t.shape
    levels = pick.shape[1]
    return pl.pallas_call(
        local_levels_kernel,
        out_shape=jax.ShapeDtypeStruct((levels - 2, rank, rank), BF16),
        in_specs=[SMEM, VMEM, VMEM, VMEM],
        out_specs=VMEM,
        scratch_shapes=[
            pltpu.VMEM((rest.shape[1] + 1, leaves, rank, rank), BF16),
            pltpu.VMEM((levels - 1, leaves // 2, rank, rank), BF16),
            pltpu.VMEM((leaves // 2, rank, rank), F32),
        ],
        compiler_params=PARAMS,
    )(pick, z, rest, basis_t)


def pair_t(side_ref, own, partner):
    is_left = side_ref[0] == 0
    left = jnp.where(is_left, own, partner)
    right = jnp.where(is_left, partner, own)
    return jnp.concatenate([left, right], axis=1)


def pair_level_kernel(side_ref, own_ref, partner_ref, out_ref, gram_ref):
    levels, rank, _ = own_ref.shape
    scale = 1.0 / math.sqrt(2 * rank)
    e_t = cholqr_t([pair_t(side_ref, own_ref[0], partner_ref[0])], gram_ref)[0].astype(BF16)
    for level in range(1, levels):
        out_ref[level - 1] = move(pair_t(side_ref, own_ref[level], partner_ref[level]), e_t, scale)


def pair_level(side, own, partner):
    levels, rank, _ = own.shape
    return pl.pallas_call(
        pair_level_kernel,
        out_shape=jax.ShapeDtypeStruct((levels - 1, rank, rank), BF16),
        in_specs=[SMEM, VMEM, VMEM],
        out_specs=VMEM,
        scratch_shapes=[pltpu.VMEM((1, rank, rank), F32)],
        compiler_params=PARAMS,
    )(side, own, partner)


def top_level_kernel(side_ref, own_ref, partner_ref, out_ref, gram_ref, full_ref):
    rows = out_ref.shape[0]
    e_t = cholqr_t([pair_t(side_ref, own_ref[0], partner_ref[0])], gram_ref)[0]
    full_ref[...] = e_t.T
    start = pl.multiple_of(side_ref[1] * rows, rows)
    out_ref[...] = full_ref[pl.ds(start, rows), :].astype(BF16)


def top_level(side, own, partner, rows):
    rank = own.shape[1]
    return pl.pallas_call(
        top_level_kernel,
        out_shape=jax.ShapeDtypeStruct((rows, rank), BF16),
        in_specs=[SMEM, VMEM, VMEM],
        out_specs=VMEM,
        scratch_shapes=[pltpu.VMEM((1, rank, rank), F32), pltpu.VMEM((2 * rank, rank), F32)],
        compiler_params=PARAMS,
    )(side, own, partner)


def plan(block_cols, leaf_ids, top_level):
    level_ids = jnp.arange(top_level, dtype=jnp.int32)
    near = block_cols[:, 2:]
    outside = (
        jnp.right_shift(leaf_ids[:, None, None], level_ids)
        != jnp.right_shift(near[:, :, None], level_ids)
    )
    drop = jnp.sum(outside.astype(jnp.int32), axis=2)
    count = near.shape[1]
    slot_ids = jnp.arange(count, dtype=jnp.int32)
    before = (drop[:, None, :] > drop[:, :, None]) | (
        (drop[:, None, :] == drop[:, :, None]) & (slot_ids[None, None, :] < slot_ids[None, :, None])
    )
    rank = jnp.sum(before.astype(jnp.int32), axis=2)
    chosen = (rank[:, None, :] == slot_ids[None, :, None]).astype(jnp.int32)
    one = jnp.ones_like(near[:, :1])
    slots = jnp.concatenate([one, jnp.sum(chosen * (slot_ids + 2), axis=2)], axis=1)
    blocks = jnp.concatenate([block_cols[:, 1:2], jnp.sum(chosen * near[:, None, :], axis=2)], axis=1)
    pick = jnp.sum((drop[:, None, :] <= level_ids[None, 1:, None]).astype(jnp.int32), axis=2)
    return slots, blocks, pick


def ring_gather(piece, size_rows):
    chips = size_rows // 2

    def ahead(value, distance):
        pairs = [
            (2 * z + k, 2 * ((z - distance) % chips) + k) for z in range(chips) for k in range(2)
        ]
        return lax.ppermute(value, "row", pairs)

    count = piece.shape[0]
    at_4 = ahead(piece, 4)
    at_2, at_6 = ahead(piece, 2), ahead(piece, -2)
    both = jnp.concatenate([piece, at_4], axis=0)
    at_1_5, at_7_3 = ahead(both, 1), ahead(both, -1)
    mine = jnp.concatenate(
        [piece, at_1_5[:count], at_2, at_7_3[count:], at_4, at_1_5[count:], at_6, at_7_3[:count]],
        axis=0,
    )
    return mine, partner_2(mine, "row", 0)


def partner_2(value, axis, stride):
    mask = 2**stride
    pairs = [(source, source ^ mask) for source in range(lax.axis_size(axis))]
    return lax.ppermute(value, axis, pairs)


def shards(front_blocks, block_cols, samples, sketch_matrix):
    leaf_dev, _, leaf_size, _ = front_blocks.shape
    rank_size = sketch_matrix.shape[1]
    size_rows, size_cols = lax.axis_size("row"), lax.axis_size("col")
    row_index = lax.axis_index("row")
    top = (leaf_dev * size_rows).bit_length() - 1
    leaf_ids = row_index * leaf_dev + jnp.arange(leaf_dev, dtype=jnp.int32)
    slots, columns, pick = plan(block_cols, leaf_ids, top)
    owner = columns // leaf_dev
    others = (owner ^ row_index) & 1
    chips = size_rows // 2
    blocks = ((owner // 2 - row_index // 2) & (chips - 1)) * leaf_dev + columns % leaf_dev

    col = lax.axis_index("col").reshape(1).astype(jnp.int32)
    parts = partial_sketch(col, samples.T, sketch_matrix, size_cols)
    sk = sum_parts(lax.all_to_all(parts, "col", 0, 0), leaf_dev)
    mine, theirs = ring_gather(sk, size_rows)

    first, rest = products(slots, blocks, others, front_blocks, mine, theirs, size_cols)
    rest = lax.all_gather(rest, "col")
    z = lax.all_to_all(first, "col", 0, 0)
    basis, basis_t = leaf_bases(z)
    carried = local_levels(pick, z, rest, basis_t)

    bit = 0
    out_rows = 4 * rank_size // size_rows
    while True:
        partner = partner_2(carried, "row", bit)
        side = jnp.stack(
            [jnp.right_shift(row_index, bit) & 1, row_index % (size_rows // 2)]
        ).astype(jnp.int32)
        if carried.shape[0] == 1:
            break
        carried = pair_level(side, carried, partner)
        bit += 1
    top_rows = top_level(side, carried, partner, out_rows)
    return basis.reshape(leaf_dev * leaf_size, rank_size), top_rows


def solution(mesh):
    placed = (P("row", None, None, None), P("row", None), P("row", "col"), P())
    return jax.shard_map(
        shards,
        mesh=mesh,
        in_specs=placed,
        out_specs=(P("row", None), P("row", None)),
        check_vma=False,
    )
```

```python
import math

import jax
import jax.numpy as jnp
from jax import lax
from jax.experimental import pallas as pl
from jax.experimental.pallas import tpu as pltpu
from jax.sharding import PartitionSpec as P

F32 = jnp.float32
BF16 = jnp.bfloat16


NN = (((1,), (0,)), ((), ()))
NT = (((1,), (1,)), ((), ()))


def split(x):
    high = x.astype(BF16)
    return high, (x - high.astype(F32)).astype(BF16)


def product(a, b, dims):
    a_high, a_low = split(a)
    b_high, b_low = split(b)

    def dot(x, y):
        return lax.dot_general(x, y, dims, preferred_element_type=F32)

    return dot(a_high, b_high) + (dot(a_high, b_low) + dot(a_low, b_high))


def mm(a, b):
    return product(a, b, NN)


def mm_t(a, b):
    return product(a, b, NT)


def dot_t(a, b):
    return lax.dot_general(a, b, (((1,), (1,)), ((), ())), preferred_element_type=F32)


def factor64(blocks, width, paired, far):
    shape = blocks[0].shape
    sub = lax.broadcasted_iota(jnp.int32, shape, 1)
    rows = list(blocks)
    out = [None] * 8
    for start in range(0, 64, width):
        own = start // 8
        below = list(range((start + width) // 8, 8))

        def spread(q):
            return [
                jnp.broadcast_to(rows[q][:, :, 64 + start + k : 65 + start + k], shape)
                for k in range(width)
            ]

        mine = spread(own)
        col = {q: list(mine) if q == own else spread(q) for q in below}
        late = [q for q in below if far and q > own + 1]
        near = [q for q in below if q not in late]
        a = [[None] * width for _ in range(width)]
        r = []
        for k in range(width):
            at = (start + k) % 8
            r.append(jnp.broadcast_to(rows[own][:, at : at + 1, :], shape))
            for i in range(k, width):
                at = (start + i) % 8
                a[i][k] = jnp.broadcast_to(mine[k][:, at : at + 1, :], shape)
        low = {q: [None] * width for q in near}
        mult = [[None] * width for _ in range(width)]
        inv = [None] * width
        scaled = [None] * width
        if paired:
            for j in range(0, width, 2):
                p, s, t = a[j][j], a[j + 1][j], a[j + 1][j + 1]
                root = lax.rsqrt(p * t - s * s)
                inv_det = root * root
                p_inv, s_inv, t_inv = t * inv_det, -(s * inv_det), p * inv_det
                m, n = {}, {}
                for k in range(j + 2, width):
                    m[k] = (t * a[k][j] - s * a[k][j + 1]) * inv_det
                    n[k] = (p * a[k][j + 1] - s * a[k][j]) * inv_det
                for k in range(j + 2, width):
                    for i in range(k, width):
                        a[i][k] = a[i][k] - (m[k] * a[i][j] + n[k] * a[i][j + 1])
                    r[k] = r[k] - (m[k] * r[j] + n[k] * r[j + 1])
                for q in near:
                    c, d = col[q][j], col[q][j + 1]
                    low[q][j] = c * p_inv + d * s_inv
                    low[q][j + 1] = c * s_inv + d * t_inv
                    for k in range(j + 2, width):
                        col[q][k] = col[q][k] - (m[k] * c + n[k] * d)
                first = lax.rsqrt(p)
                scaled[j] = r[j] * first
                scaled[j + 1] = (r[j + 1] - (s * (first * first)) * r[j]) * ((p * first) * root)
        else:
            for j in range(width):
                root = lax.rsqrt(a[j][j])
                inv[j] = root * root
                for k in range(j + 1, width):
                    mult[j][k] = a[k][j] * inv[j]
                for k in range(j + 1, width):
                    for i in range(k, width):
                        a[i][k] = a[i][k] - mult[j][k] * a[i][j]
                    r[k] = r[k] - mult[j][k] * r[j]
                for q in near:
                    low[q][j] = col[q][j] * inv[j]
                    for k in range(j + 1, width):
                        col[q][k] = col[q][k] - mult[j][k] * col[q][j]
                scaled[j] = r[j] * root
        for j in range(width):
            at = (start + j) % 8
            out[own] = scaled[j] if at == 0 else jnp.where(sub == at, scaled[j], out[own])
        solved = [None] * width
        if late:
            for j in reversed(range(width)):
                value = r[j] * inv[j]
                for k in range(j + 1, width):
                    value = value - mult[j][k] * solved[k]
                solved[j] = value
        for q in below:
            if q in late:
                terms = [col[q][j] * solved[j] for j in range(width)]
            else:
                terms = [low[q][j] * r[j] for j in range(width)]
            while len(terms) > 1:
                terms = [terms[i] + terms[i + 1] for i in range(0, len(terms), 2)]
            rows[q] = rows[q] - terms[0]
    return out


FORMS = {1: (8, True, False), 2: (8, False, False), 4: (4, False, True)}


def inverse64(wide):
    lane = lax.broadcasted_iota(jnp.int32, (64, 128), 1)
    row = lax.broadcasted_iota(jnp.int32, (64, 128), 0)
    eye = (lane == row).astype(F32)
    full = [jnp.where(lane >= 64, w, eye) for w in wide]
    form = FORMS.get(len(wide), (4, False, True))
    out = factor64([jnp.stack([f[8 * i : 8 * i + 8] for f in full]) for i in range(8)], *form)
    return [jnp.concatenate([o[b] for o in out], axis=0) for b in range(len(wide))]


def inverse128(blocks):
    n = range(len(blocks))
    lane = lax.broadcasted_iota(jnp.int32, (64, 128), 1)
    row = lax.broadcasted_iota(jnp.int32, (64, 128), 0)
    first = inverse64([pltpu.roll(b[:64], 64, 1) for b in blocks])
    first = [jnp.where(lane < 64, f, 0.0) for f in first]
    right = [mm(first[i][:, :64], blocks[i][:64]) for i in n]
    left = [mm_t(blocks[i][64:, :64], first[i][:, :64]) for i in n]
    schur = [blocks[i][64:] - mm(left[i], right[i]) for i in n]
    mixed = [mm(left[i], first[i]) for i in n]
    second = inverse64(schur)
    eye = (lane == row + 64).astype(F32)
    low = [mm(second[i][:, :64], jnp.where(lane < 64, -mixed[i], eye)) for i in n]
    return [jnp.concatenate([first[i], low[i]], axis=0) for i in n]


def cholqr_t(z_ts, gram_ref):
    n = range(len(z_ts))
    half = z_ts[0].shape[0] // 2
    for i in n:
        gram_ref[i] = dot_t(z_ts[i], z_ts[i])
    first = inverse128([gram_ref[i, 0:half, 0:half] for i in n])
    right = [mm(first[i], gram_ref[i, 0:half, half:]) for i in n]
    left = [mm_t(gram_ref[i, half:, 0:half], first[i]) for i in n]
    schur = [gram_ref[i, half:, half:] - mm(left[i], right[i]) for i in n]
    top = []
    for i in n:
        high, low = split(first[i])
        z_1 = z_ts[i][:half]
        top.append(
            jnp.dot(high, z_1, preferred_element_type=F32)
            + jnp.dot(low, z_1, preferred_element_type=F32)
        )
    below = [z_ts[i][half:].astype(F32) - mm(left[i], top[i]) for i in n]
    second = inverse128(schur)
    scale = math.sqrt(z_ts[0].shape[1])
    return [jnp.concatenate([top[i], mm(second[i], below[i])], axis=0) * scale for i in n]


VMEM = pl.BlockSpec(memory_space=pltpu.MemorySpace.VMEM)
SMEM = pl.BlockSpec(memory_space=pltpu.MemorySpace.SMEM)
ANY = pl.BlockSpec(memory_space=pl.ANY)
PARAMS = pltpu.CompilerParams(vmem_limit_bytes=48 << 20)


def partial_kernel(col_ref, x_t_ref, w_ref, out_ref):
    depth = x_t_ref.shape[0]
    start = pl.multiple_of(col_ref[0] * depth, depth)
    part = lax.dot_general(
        w_ref[pl.ds(start, depth), :], x_t_ref[...],
        (((0,), (0,)), ((), ())), preferred_element_type=F32,
    )
    out_ref[...] = part.astype(BF16).reshape(out_ref.shape)


def partial_sketch(col, x_t, w, size_cols):
    shape = (size_cols, w.shape[1] // size_cols, x_t.shape[1])
    return pl.pallas_call(
        partial_kernel,
        out_shape=jax.ShapeDtypeStruct(shape, BF16),
        in_specs=[SMEM, VMEM, VMEM],
        out_specs=VMEM,
        compiler_params=PARAMS,
    )(col, x_t, w)


def sum_kernel(parts_ref, out_ref):
    leaves, _, size = out_ref.shape
    for m in range(leaves):
        at = slice(m * size, (m + 1) * size)
        total = parts_ref[0, :, at].astype(F32)
        for s in range(1, parts_ref.shape[0]):
            total = total + parts_ref[s, :, at].astype(F32)
        out_ref[m] = total.astype(BF16)


def sum_parts(parts, leaves):
    _, cols, rows = parts.shape
    return pl.pallas_call(
        sum_kernel,
        out_shape=jax.ShapeDtypeStruct((leaves, cols, rows // leaves), BF16),
        in_specs=[VMEM],
        out_specs=VMEM,
        compiler_params=PARAMS,
    )(parts)


def products_kernel(
    slot_ref, block_ref, other_ref, front_ref, mine_ref, theirs_ref, out_ref, held_ref, sems
):
    leaves, steps = slot_ref.shape
    copies_in = [
        [
            pltpu.make_async_copy(
                front_ref.at[m, slot_ref[m, s]], held_ref.at[m, s], sems.at[m, s]
            )
            for s in range(steps)
        ]
        for m in range(leaves)
    ]
    for m in range(leaves):
        for s in range(steps):
            copies_in[m][s].start()
    cols = mine_ref.shape[1]
    copies = out_ref.shape[0] // leaves
    for m in range(leaves):
        total = None
        for s in range(steps):
            block = block_ref[m, s]
            sk = jnp.where(other_ref[m, s] == 0, mine_ref[block], theirs_ref[block])
            wide = jnp.concatenate([sk] * (steps - s) + [jnp.zeros_like(sk)] * s, axis=0)
            copies_in[m][s].wait()
            part = dot_t(held_ref[m, s], wide)
            total = part if total is None else total + part
        sums = total.T.astype(BF16).reshape(steps, cols, total.shape[0])
        for d in range(copies):
            out_ref[m * copies + d] = sums


def products(slots, blocks, others, front, mine, theirs, peers):
    leaves, _, size, _ = front.shape
    steps = slots.shape[1]
    cols = mine.shape[1]
    return pl.pallas_call(
        products_kernel,
        out_shape=jax.ShapeDtypeStruct((peers, steps, cols, size), BF16),
        in_specs=[SMEM, SMEM, SMEM, ANY, VMEM, VMEM],
        out_specs=VMEM,
        scratch_shapes=[
            pltpu.VMEM((leaves, steps, size, size), BF16),
            pltpu.SemaphoreType.DMA((leaves, steps)),
        ],
        compiler_params=PARAMS,
    )(slots, blocks, others, front, mine, theirs)


def leaf_kernel(place_ref, pick_ref, z_ref, part_ref, first_ref, rest_ref, gram_ref, basis_ref):
    sources, _, cols, size = z_ref.shape
    rank = sources * cols
    leaf = place_ref[0]
    q_t = cholqr_t([z_ref[:, 0].reshape(rank, size)], gram_ref)[0]
    basis_t = q_t.astype(BF16)
    scale = 1.0 / math.sqrt(size)
    for level in range(pick_ref.shape[1]):
        proj = move(z_ref[:, pick_ref[leaf, level]].reshape(rank, size), basis_t, scale)
        if level == 0:
            first_ref[...] = proj
        else:
            rest_ref[level - 1] = proj
    basis_ref[...] = q_t.T
    rows = part_ref.shape[0]
    start = pl.multiple_of(place_ref[1] * rows, rows)
    part_ref[...] = basis_ref[pl.ds(start, rows), :].astype(BF16)


def leaf_level(place, pick, z, parts):
    sources, _, cols, size = z.shape
    rank = sources * cols
    return pl.pallas_call(
        leaf_kernel,
        out_shape=(
            jax.ShapeDtypeStruct((size // parts, rank), BF16),
            jax.ShapeDtypeStruct((rank, rank), BF16),
            jax.ShapeDtypeStruct((pick.shape[1] - 1, rank, rank), BF16),
        ),
        in_specs=[SMEM, SMEM, VMEM],
        out_specs=(VMEM, VMEM, VMEM),
        scratch_shapes=[pltpu.VMEM((1, rank, rank), F32), pltpu.VMEM((size, rank), F32)],
        compiler_params=PARAMS,
    )(place, pick, z)


def move(stacked, transfer, scale):
    return (dot_t(stacked, transfer) * scale).astype(BF16)


def pair_t(side_ref, own, partner):
    is_left = side_ref[0] == 0
    left = jnp.where(is_left, own, partner)
    right = jnp.where(is_left, partner, own)
    return jnp.concatenate([left, right], axis=1)


def transfer_kernel(side_ref, own_ref, partner_ref, out_ref, gram_ref):
    z_t = pair_t(side_ref, own_ref[...], partner_ref[...])
    out_ref[...] = cholqr_t([z_t], gram_ref)[0].astype(BF16)


def transfer(side, own, partner):
    rank = own.shape[0]
    return pl.pallas_call(
        transfer_kernel,
        out_shape=jax.ShapeDtypeStruct((rank, 2 * rank), BF16),
        in_specs=[SMEM, VMEM, VMEM],
        out_specs=VMEM,
        scratch_shapes=[pltpu.VMEM((1, rank, rank), F32)],
        compiler_params=PARAMS,
    )(side, own, partner)


def moves_kernel(side_ref, e_t_ref, own_ref, partner_ref, first_ref, *rest_ref):
    levels, rank, _ = own_ref.shape
    scale = 1.0 / math.sqrt(2 * rank)
    for level in range(levels):
        moved = move(pair_t(side_ref, own_ref[level], partner_ref[level]), e_t_ref[...], scale)
        if level == 0:
            first_ref[...] = moved
        else:
            rest_ref[0][level - 1] = moved


def moves(side, e_t, own, partner):
    levels, rank, _ = own.shape
    shapes = [jax.ShapeDtypeStruct((rank, rank), BF16)]
    if levels > 1:
        shapes.append(jax.ShapeDtypeStruct((levels - 1, rank, rank), BF16))
    out = pl.pallas_call(
        moves_kernel,
        out_shape=tuple(shapes),
        in_specs=[SMEM, VMEM, VMEM, VMEM],
        out_specs=(VMEM,) * len(shapes),
        compiler_params=PARAMS,
    )(side, e_t, own, partner)
    return out if levels > 1 else (out[0], own[:0])


def top_level_kernel(side_ref, own_ref, partner_ref, basis_ref, out_ref, basis_out_ref, gram_ref, full_ref, sem):
    copy = pltpu.make_async_copy(basis_ref, basis_out_ref, sem)
    copy.start()
    rows = out_ref.shape[0]
    e_t = cholqr_t([pair_t(side_ref, own_ref[...], partner_ref[...])], gram_ref)[0]
    full_ref[...] = e_t.T
    start = pl.multiple_of(side_ref[1] * rows, rows)
    out_ref[...] = full_ref[pl.ds(start, rows), :].astype(BF16)
    copy.wait()


def top_level(side, own, partner, rows, basis):
    rank = own.shape[0]
    return pl.pallas_call(
        top_level_kernel,
        out_shape=(
            jax.ShapeDtypeStruct((rows, rank), BF16),
            jax.ShapeDtypeStruct(basis.shape, BF16),
        ),
        in_specs=[SMEM, VMEM, VMEM, ANY],
        out_specs=(VMEM, ANY),
        scratch_shapes=[
            pltpu.VMEM((1, rank, rank), F32),
            pltpu.VMEM((2 * rank, rank), F32),
            pltpu.SemaphoreType.DMA(()),
        ],
        compiler_params=PARAMS,
    )(side, own, partner, basis)


def plan(block_cols, leaf_ids, top_level):
    level_ids = jnp.arange(top_level, dtype=jnp.int32)
    near = block_cols[:, 2:]
    outside = (
        jnp.right_shift(leaf_ids[:, None, None], level_ids)
        != jnp.right_shift(near[:, :, None], level_ids)
    )
    drop = jnp.sum(outside.astype(jnp.int32), axis=2)
    count = near.shape[1]
    slot_ids = jnp.arange(count, dtype=jnp.int32)
    before = (drop[:, None, :] > drop[:, :, None]) | (
        (drop[:, None, :] == drop[:, :, None]) & (slot_ids[None, None, :] < slot_ids[None, :, None])
    )
    rank = jnp.sum(before.astype(jnp.int32), axis=2)
    chosen = (rank[:, None, :] == slot_ids[None, :, None]).astype(jnp.int32)
    one = jnp.ones_like(near[:, :1])
    slots = jnp.concatenate([one, jnp.sum(chosen * (slot_ids + 2), axis=2)], axis=1)
    blocks = jnp.concatenate([block_cols[:, 1:2], jnp.sum(chosen * near[:, None, :], axis=2)], axis=1)
    pick = jnp.sum((drop[:, None, :] <= level_ids[None, 1:, None]).astype(jnp.int32), axis=2)
    return slots, blocks, pick


def ring_gather(piece, size_rows):
    chips = size_rows // 2

    def ahead(value, distance):
        pairs = [
            (2 * z + k, 2 * ((z - distance) % chips) + k) for z in range(chips) for k in range(2)
        ]
        return lax.ppermute(value, "row", pairs)

    count = piece.shape[0]
    at_4, at_2, at_6 = lax.optimization_barrier(
        (ahead(piece, 4), ahead(piece, 2), ahead(piece, -2))
    )
    both = jnp.concatenate([piece, at_4], axis=0)
    at_1_5, at_7_3 = ahead(both, 1), ahead(both, -1)
    mine = jnp.concatenate(
        [piece, at_1_5[:count], at_2, at_7_3[count:], at_4, at_1_5[count:], at_6, at_7_3[:count]],
        axis=0,
    )
    return mine, partner_2(mine, "row", 0)


def partner_2(value, axis, stride):
    mask = 2**stride
    pairs = [(source, source ^ mask) for source in range(lax.axis_size(axis))]
    return lax.ppermute(value, axis, pairs)


def shards(front_blocks, block_cols, samples, sketch_matrix):
    leaf_dev, _, leaf_size, _ = front_blocks.shape
    rank_size = sketch_matrix.shape[1]
    size_rows, size_cols = lax.axis_size("row"), lax.axis_size("col")
    row_index = lax.axis_index("row")
    top = (leaf_dev * size_rows).bit_length() - 1
    leaf_ids = row_index * leaf_dev + jnp.arange(leaf_dev, dtype=jnp.int32)
    slots, columns, pick = plan(block_cols, leaf_ids, top)
    owner = columns // leaf_dev
    others = (owner ^ row_index) & 1
    chips = size_rows // 2
    blocks = ((owner // 2 - row_index // 2) & (chips - 1)) * leaf_dev + columns % leaf_dev

    col = lax.axis_index("col").reshape(1).astype(jnp.int32)
    parts = partial_sketch(col, samples.T, sketch_matrix, size_cols)
    sk = sum_parts(lax.all_to_all(parts, "col", 0, 0), leaf_dev)
    mine, theirs = ring_gather(sk, size_rows)

    sums = products(slots, blocks, others, front_blocks, mine, theirs, size_cols)
    z = lax.all_to_all(sums, "col", 0, 0)
    parts = size_cols // leaf_dev
    col_index = lax.axis_index("col")
    place = jnp.stack([col_index // parts, col_index % parts]).astype(jnp.int32)
    basis, first, rest = leaf_level(place, pick, z, parts)
    basis = lax.all_gather(basis, "col").reshape(leaf_dev * leaf_size, rank_size)
    for bit in range(leaf_dev.bit_length() - 1):
        stride = (parts << bit).bit_length() - 1
        side = (jnp.right_shift(col_index, stride) & 1).reshape(1).astype(jnp.int32)
        theirs, rest = lax.optimization_barrier((partner_2(first, "col", stride), rest))
        e_t = transfer(side, first, theirs)
        first, rest = moves(side, e_t, rest, partner_2(rest, "col", stride))
    bit = 0
    while rest.shape[0] > 0:
        side = (jnp.right_shift(row_index, bit) & 1).reshape(1).astype(jnp.int32)
        theirs, rest = lax.optimization_barrier((partner_2(first, "row", bit), rest))
        e_t = transfer(side, first, theirs)
        first, rest = moves(side, e_t, rest, partner_2(rest, "row", bit))
        bit += 1
    side = jnp.stack(
        [jnp.right_shift(row_index, bit) & 1, row_index % (size_rows // 2)]
    ).astype(jnp.int32)
    top_rows, basis = top_level(
        side, first, partner_2(first, "row", bit), 4 * rank_size // size_rows, basis
    )
    return basis, top_rows


def solution(mesh):
    placed = (P("row", None, None, None), P("row", None), P("row", "col"), P())
    return jax.shard_map(
        shards,
        mesh=mesh,
        in_specs=placed,
        out_specs=(P("row", None), P("row", None)),
        check_vma=False,
    )
```

```python
import math

import jax
import jax.numpy as jnp
from jax import lax
from jax.experimental import pallas as pl
from jax.experimental.pallas import tpu as pltpu
from jax.sharding import PartitionSpec as P

F32 = jnp.float32
BF16 = jnp.bfloat16


NN = (((1,), (0,)), ((), ()))
NT = (((1,), (1,)), ((), ()))


def split(x):
    high = x.astype(BF16)
    return high, (x - high.astype(F32)).astype(BF16)


def product(a, b, dims):
    a_high, a_low = split(a)
    b_high, b_low = split(b)

    def dot(x, y):
        return lax.dot_general(x, y, dims, preferred_element_type=F32)

    return dot(a_high, b_high) + (dot(a_high, b_low) + dot(a_low, b_high))


def mm(a, b):
    return product(a, b, NN)


def mm_t(a, b):
    return product(a, b, NT)


def dot_t(a, b):
    return lax.dot_general(a, b, (((1,), (1,)), ((), ())), preferred_element_type=F32)


def factor64(blocks, width, paired, far):
    shape = blocks[0].shape
    sub = lax.broadcasted_iota(jnp.int32, shape, 1)
    rows = list(blocks)
    out = [None] * 8
    ahead = None
    for start in range(0, 64, width):
        own = start // 8
        below = list(range((start + width) // 8, 8))

        def spread(q):
            return [
                jnp.broadcast_to(rows[q][:, :, 64 + start + k : 65 + start + k], shape)
                for k in range(width)
            ]

        mine = ahead if ahead is not None else spread(own)
        ahead = None
        col = {q: list(mine) if q == own else spread(q) for q in below}
        late = [q for q in below if far and q > own + 1]
        near = [q for q in below if q not in late]
        a = [[None] * width for _ in range(width)]
        r = []
        for k in range(width):
            at = (start + k) % 8
            r.append(jnp.broadcast_to(rows[own][:, at : at + 1, :], shape))
            for i in range(k, width):
                at = (start + i) % 8
                a[i][k] = jnp.broadcast_to(mine[k][:, at : at + 1, :], shape)
        low = {q: [None] * width for q in near}
        step = own + 1
        if paired and step in near:
            ahead = [
                jnp.broadcast_to(rows[step][:, :, 72 + start + k : 73 + start + k], shape)
                for k in range(8)
            ]
        mult = [[None] * width for _ in range(width)]
        inv = [None] * width
        scaled = [None] * width
        if paired:
            for j in range(0, width, 2):
                p, s, t = a[j][j], a[j + 1][j], a[j + 1][j + 1]
                root = lax.rsqrt(p * t - s * s)
                inv_det = root * root
                p_inv, s_inv, t_inv = t * inv_det, -(s * inv_det), p * inv_det
                m, n = {}, {}
                for k in range(j + 2, width):
                    m[k] = (t * a[k][j] - s * a[k][j + 1]) * inv_det
                    n[k] = (p * a[k][j + 1] - s * a[k][j]) * inv_det
                for k in range(j + 2, width):
                    for i in range(k, width):
                        a[i][k] = a[i][k] - (m[k] * a[i][j] + n[k] * a[i][j + 1])
                    r[k] = r[k] - (m[k] * r[j] + n[k] * r[j + 1])
                for q in near:
                    c, d = col[q][j], col[q][j + 1]
                    low[q][j] = c * p_inv + d * s_inv
                    low[q][j + 1] = c * s_inv + d * t_inv
                    for k in range(j + 2, width):
                        col[q][k] = col[q][k] - (m[k] * c + n[k] * d)
                    if q == step:
                        for k in range(8):
                            c_k = jnp.broadcast_to(c[:, k : k + 1, :], shape)
                            d_k = jnp.broadcast_to(d[:, k : k + 1, :], shape)
                            ahead[k] = ahead[k] - (low[q][j] * c_k + low[q][j + 1] * d_k)
                first = lax.rsqrt(p)
                scaled[j] = r[j] * first
                scaled[j + 1] = (r[j + 1] - (s * (first * first)) * r[j]) * ((p * first) * root)
        else:
            for j in range(width):
                root = lax.rsqrt(a[j][j])
                inv[j] = root * root
                for k in range(j + 1, width):
                    mult[j][k] = a[k][j] * inv[j]
                for k in range(j + 1, width):
                    for i in range(k, width):
                        a[i][k] = a[i][k] - mult[j][k] * a[i][j]
                    r[k] = r[k] - mult[j][k] * r[j]
                for q in near:
                    low[q][j] = col[q][j] * inv[j]
                    for k in range(j + 1, width):
                        col[q][k] = col[q][k] - mult[j][k] * col[q][j]
                scaled[j] = r[j] * root
        for j in range(width):
            at = (start + j) % 8
            out[own] = scaled[j] if at == 0 else jnp.where(sub == at, scaled[j], out[own])
        solved = [None] * width
        if late:
            for j in reversed(range(width)):
                value = r[j] * inv[j]
                for k in range(j + 1, width):
                    value = value - mult[j][k] * solved[k]
                solved[j] = value
        for q in below:
            if q in late:
                terms = [col[q][j] * solved[j] for j in range(width)]
            else:
                terms = [low[q][j] * r[j] for j in range(width)]
            while len(terms) > 1:
                terms = [terms[i] + terms[i + 1] for i in range(0, len(terms), 2)]
            rows[q] = rows[q] - terms[0]
    return out


FORMS = {1: (8, True, False), 2: (8, False, False), 4: (4, False, True)}


def inverse64(wide):
    lane = lax.broadcasted_iota(jnp.int32, (64, 128), 1)
    row = lax.broadcasted_iota(jnp.int32, (64, 128), 0)
    eye = (lane == row).astype(F32)
    full = [jnp.where(lane >= 64, w, eye) for w in wide]
    form = FORMS.get(len(wide), (4, False, True))
    out = factor64([jnp.stack([f[8 * i : 8 * i + 8] for f in full]) for i in range(8)], *form)
    return [jnp.concatenate([o[b] for o in out], axis=0) for b in range(len(wide))]


def inverse128(blocks):
    n = range(len(blocks))
    lane = lax.broadcasted_iota(jnp.int32, (64, 128), 1)
    row = lax.broadcasted_iota(jnp.int32, (64, 128), 0)
    first = inverse64([pltpu.roll(b[:64], 64, 1) for b in blocks])
    first = [jnp.where(lane < 64, f, 0.0) for f in first]
    right = [mm(first[i][:, :64], blocks[i][:64]) for i in n]
    left = [mm_t(blocks[i][64:, :64], first[i][:, :64]) for i in n]
    schur = [blocks[i][64:] - mm(left[i], right[i]) for i in n]
    mixed = [mm(left[i], first[i]) for i in n]
    second = inverse64(schur)
    eye = (lane == row + 64).astype(F32)
    low = [mm(second[i][:, :64], jnp.where(lane < 64, -mixed[i], eye)) for i in n]
    return [jnp.concatenate([first[i], low[i]], axis=0) for i in n]


def cholqr_t(z_ts, gram_ref, between=None):
    n = range(len(z_ts))
    half = z_ts[0].shape[0] // 2
    for i in n:
        gram_ref[i] = dot_t(z_ts[i], z_ts[i])
    first = inverse128([gram_ref[i, 0:half, 0:half] for i in n])
    right = [mm(first[i], gram_ref[i, 0:half, half:]) for i in n]
    left = [mm_t(gram_ref[i, half:, 0:half], first[i]) for i in n]
    schur = [gram_ref[i, half:, half:] - mm(left[i], right[i]) for i in n]
    top = []
    for i in n:
        high, low = split(first[i])
        z_1 = z_ts[i][:half]
        top.append(
            jnp.dot(high, z_1, preferred_element_type=F32)
            + jnp.dot(low, z_1, preferred_element_type=F32)
        )
    below = [z_ts[i][half:].astype(F32) - mm(left[i], top[i]) for i in n]
    if between is not None:
        between()
    second = inverse128(schur)
    scale = math.sqrt(z_ts[0].shape[1])
    return [jnp.concatenate([top[i], mm(second[i], below[i])], axis=0) * scale for i in n]


VMEM = pl.BlockSpec(memory_space=pltpu.MemorySpace.VMEM)
SMEM = pl.BlockSpec(memory_space=pltpu.MemorySpace.SMEM)
HBM = pl.BlockSpec(memory_space=pltpu.MemorySpace.HBM)
PARAMS = pltpu.CompilerParams(vmem_limit_bytes=48 << 20)


def in_hbm(x):
    return pltpu.with_memory_space_constraint(x, pltpu.MemorySpace.HBM)


def partial_kernel(col_ref, x_t_ref, w_ref, out_ref):
    part = lax.dot_general(
        w_ref[...], x_t_ref[...], (((0,), (0,)), ((), ())), preferred_element_type=F32
    )
    out_ref[...] = part.astype(BF16).reshape(out_ref.shape)


def partial_sketch(col, x_t, w, size_cols):
    depth, rows = x_t.shape
    rank = w.shape[1]
    shape = (size_cols, rank // size_cols, rows)
    return pl.pallas_call(
        partial_kernel,
        out_shape=jax.ShapeDtypeStruct(shape, BF16),
        grid_spec=pltpu.PrefetchScalarGridSpec(
            num_scalar_prefetch=1,
            grid=(1,),
            in_specs=[
                pl.BlockSpec((depth, rows), lambda i, col: (0, 0)),
                pl.BlockSpec((depth, rank), lambda i, col: (col[0], 0)),
            ],
            out_specs=pl.BlockSpec(shape, lambda i, col: (0, 0, 0)),
        ),
        compiler_params=PARAMS,
    )(col, x_t, w)


def sum_kernel(parts_ref, out_ref):
    leaves, _, size = out_ref.shape
    for m in range(leaves):
        at = slice(m * size, (m + 1) * size)
        total = parts_ref[0, :, at].astype(F32)
        for s in range(1, parts_ref.shape[0]):
            total = total + parts_ref[s, :, at].astype(F32)
        out_ref[m] = total.astype(BF16)


def sum_parts(parts, leaves):
    _, cols, rows = parts.shape
    return pl.pallas_call(
        sum_kernel,
        out_shape=jax.ShapeDtypeStruct((leaves, cols, rows // leaves), BF16),
        in_specs=[VMEM],
        out_specs=VMEM,
        compiler_params=PARAMS,
    )(parts)


def products_kernel(
    slot_ref, block_ref, other_ref, front_ref, mine_ref, theirs_ref, out_ref, held_ref, sems
):
    leaves, steps = slot_ref.shape
    copies_in = [
        [
            pltpu.make_async_copy(
                front_ref.at[m, slot_ref[m, s]], held_ref.at[m, s], sems.at[m, s]
            )
            for s in range(steps)
        ]
        for m in range(leaves)
    ]
    for m in range(leaves):
        for s in range(steps):
            copies_in[m][s].start()
    cols = mine_ref.shape[1]
    copies = out_ref.shape[0] // leaves
    for m in range(leaves):
        total = None
        for s in range(steps):
            block = block_ref[m, s]
            sk = jnp.where(other_ref[m, s] == 0, mine_ref[block], theirs_ref[block])
            wide = jnp.concatenate([sk] * (steps - s) + [jnp.zeros_like(sk)] * s, axis=0)
            copies_in[m][s].wait()
            part = dot_t(wide, held_ref[m, s])
            total = part if total is None else total + part
        sums = total.astype(BF16).reshape(steps, cols, total.shape[1])
        for d in range(copies):
            out_ref[m * copies + d] = sums


def products(slots, blocks, others, front, mine, theirs, peers):
    leaves, _, size, _ = front.shape
    steps = slots.shape[1]
    cols = mine.shape[1]
    return pl.pallas_call(
        products_kernel,
        out_shape=jax.ShapeDtypeStruct((peers, steps, cols, size), BF16),
        in_specs=[SMEM, SMEM, SMEM, HBM, VMEM, VMEM],
        out_specs=VMEM,
        scratch_shapes=[
            pltpu.VMEM((leaves, steps, size, size), BF16),
            pltpu.SemaphoreType.DMA((leaves, steps)),
        ],
        compiler_params=PARAMS,
    )(slots, blocks, others, front, mine, theirs)


def rows_of(q_t, start, count):
    shape = (count, q_t.shape[1])
    lane = lax.broadcasted_iota(jnp.int32, shape, 1)
    chosen = lane == lax.broadcasted_iota(jnp.int32, shape, 0) + start
    return dot_t(chosen.astype(F32).astype(BF16), q_t).astype(BF16)


def leaf_kernel(place_ref, pick_ref, z_ref, part_ref, first_ref, second_ref, rest_ref, gram_ref):
    sources, _, cols, size = z_ref.shape
    rank = sources * cols
    leaf = place_ref[0]
    q_t = cholqr_t([z_ref[:, 0].reshape(rank, size)], gram_ref)[0]
    basis_t = q_t.astype(BF16)
    scale = 1.0 / math.sqrt(size)
    for level in range(pick_ref.shape[1]):
        proj = move(z_ref[:, pick_ref[leaf, level]].reshape(rank, size), basis_t, scale)
        if level == 0:
            first_ref[0] = proj
        elif level == 1:
            second_ref[0] = proj
        else:
            rest_ref[level - 2] = proj
    part_ref[...] = rows_of(basis_t, place_ref[1] * part_ref.shape[0], part_ref.shape[0])


def leaf_level(place, pick, z, parts):
    sources, _, cols, size = z.shape
    rank = sources * cols
    return pl.pallas_call(
        leaf_kernel,
        out_shape=(
            jax.ShapeDtypeStruct((size // parts, rank), BF16),
            jax.ShapeDtypeStruct((1, rank, rank), BF16),
            jax.ShapeDtypeStruct((1, rank, rank), BF16),
            jax.ShapeDtypeStruct((pick.shape[1] - 2, rank, rank), BF16),
        ),
        in_specs=[SMEM, SMEM, VMEM],
        out_specs=(VMEM, VMEM, VMEM, VMEM),
        scratch_shapes=[pltpu.VMEM((1, rank, rank), F32)],
        compiler_params=PARAMS,
    )(place, pick, z)


def move(stacked, transfer, scale):
    return (dot_t(stacked, transfer) * scale).astype(BF16)


def pair_t(side_ref, own, partner):
    is_left = side_ref[0] == 0
    left = jnp.where(is_left, own, partner)
    right = jnp.where(is_left, partner, own)
    return jnp.concatenate([left, right], axis=1)


def transfer_kernel(side_ref, own_ref, partner_ref, out_ref, gram_ref):
    z_t = pair_t(side_ref, own_ref[...], partner_ref[...])
    out_ref[...] = cholqr_t([z_t], gram_ref)[0].astype(BF16)


def transfer(side, own, partner):
    rank = own.shape[0]
    return pl.pallas_call(
        transfer_kernel,
        out_shape=jax.ShapeDtypeStruct((rank, 2 * rank), BF16),
        in_specs=[SMEM, VMEM, VMEM],
        out_specs=VMEM,
        scratch_shapes=[pltpu.VMEM((1, rank, rank), F32)],
        compiler_params=PARAMS,
    )(side, own, partner)


def moves_kernel(side_ref, e_t_ref, own_ref, partner_ref, out_ref):
    levels, rank, _ = own_ref.shape
    scale = 1.0 / math.sqrt(2 * rank)
    for level in range(levels):
        z_t = pair_t(side_ref, own_ref[level], partner_ref[level])
        out_ref[level] = move(z_t, e_t_ref[...], scale)


def moves(side, e_t, own, partner):
    return pl.pallas_call(
        moves_kernel,
        out_shape=jax.ShapeDtypeStruct(own.shape, BF16),
        in_specs=[SMEM, VMEM, VMEM, VMEM],
        out_specs=VMEM,
        compiler_params=PARAMS,
    )(side, e_t, own, partner)


def climb(side, groups, axis, stride):
    first, *groups = lax.optimization_barrier((partner_2(groups[0], axis, stride), *groups))
    theirs = [first] + [partner_2(group, axis, stride) for group in groups[1:]]
    e_t = transfer(side, groups[0][0], theirs[0][0])
    moved = [moves(side, e_t, own, other) for own, other in zip(groups[1:], theirs[1:])]
    if len(moved) == 1 or moved[1].shape[0] == 1:
        return moved
    return [moved[0], moved[1][:1], moved[1][1:]]


def top_level_kernel(
    side_ref, own_ref, partner_ref, basis_ref, out_ref, basis_out_ref, gram_ref, held_ref, sems
):
    copy_in = pltpu.make_async_copy(basis_ref, held_ref, sems.at[0])
    copy_out = pltpu.make_async_copy(held_ref, basis_out_ref, sems.at[1])

    def pass_on():
        copy_in.wait()
        copy_out.start()

    copy_in.start()
    rows = out_ref.shape[0]
    z_t = pair_t(side_ref, own_ref[...], partner_ref[...])
    e_t = cholqr_t([z_t], gram_ref, pass_on)[0]
    out_ref[...] = rows_of(e_t.astype(BF16), side_ref[1] * rows, rows)
    copy_out.wait()


def top_level(side, own, partner, rows, basis):
    rank = own.shape[0]
    return pl.pallas_call(
        top_level_kernel,
        out_shape=(
            jax.ShapeDtypeStruct((rows, rank), BF16),
            jax.ShapeDtypeStruct(basis.shape, BF16),
        ),
        in_specs=[SMEM, VMEM, VMEM, HBM],
        out_specs=(VMEM, HBM),
        scratch_shapes=[
            pltpu.VMEM((1, rank, rank), F32),
            pltpu.VMEM(basis.shape, BF16),
            pltpu.SemaphoreType.DMA((2,)),
        ],
        compiler_params=PARAMS,
    )(side, own, partner, basis)


def plan(block_cols, leaf_ids, top_level):
    level_ids = jnp.arange(top_level, dtype=jnp.int32)
    near = block_cols[:, 2:]
    outside = (
        jnp.right_shift(leaf_ids[:, None, None], level_ids)
        != jnp.right_shift(near[:, :, None], level_ids)
    )
    drop = jnp.sum(outside.astype(jnp.int32), axis=2)
    count = near.shape[1]
    slot_ids = jnp.arange(count, dtype=jnp.int32)
    before = (drop[:, None, :] > drop[:, :, None]) | (
        (drop[:, None, :] == drop[:, :, None]) & (slot_ids[None, None, :] < slot_ids[None, :, None])
    )
    rank = jnp.sum(before.astype(jnp.int32), axis=2)
    chosen = (rank[:, None, :] == slot_ids[None, :, None]).astype(jnp.int32)
    one = jnp.ones_like(near[:, :1])
    slots = jnp.concatenate([one, jnp.sum(chosen * (slot_ids + 2), axis=2)], axis=1)
    blocks = jnp.concatenate([block_cols[:, 1:2], jnp.sum(chosen * near[:, None, :], axis=2)], axis=1)
    pick = jnp.sum((drop[:, None, :] <= level_ids[None, 1:, None]).astype(jnp.int32), axis=2)
    return slots, blocks, pick


def ring_gather(piece, size_rows):
    chips = size_rows // 2

    def ahead(value, distance):
        pairs = [
            (2 * z + k, 2 * ((z - distance) % chips) + k) for z in range(chips) for k in range(2)
        ]
        return lax.ppermute(value, "row", pairs)

    count = piece.shape[0]
    at_4, at_2, at_6 = lax.optimization_barrier(
        (ahead(piece, 4), ahead(piece, 2), ahead(piece, -2))
    )
    both = jnp.concatenate([piece, at_4], axis=0)
    at_1_5, at_7_3 = ahead(both, 1), ahead(both, -1)
    mine = jnp.concatenate(
        [piece, at_1_5[:count], at_2, at_7_3[count:], at_4, at_1_5[count:], at_6, at_7_3[:count]],
        axis=0,
    )
    return mine, partner_2(mine, "row", 0)


def partner_2(value, axis, stride):
    mask = 2**stride
    pairs = [(source, source ^ mask) for source in range(lax.axis_size(axis))]
    return lax.ppermute(value, axis, pairs)


def shards(front_blocks, block_cols, samples, sketch_matrix):
    leaf_dev, _, leaf_size, _ = front_blocks.shape
    rank_size = sketch_matrix.shape[1]
    size_rows, size_cols = lax.axis_size("row"), lax.axis_size("col")
    row_index = lax.axis_index("row")
    top = (leaf_dev * size_rows).bit_length() - 1
    leaf_ids = row_index * leaf_dev + jnp.arange(leaf_dev, dtype=jnp.int32)
    slots, columns, pick = plan(block_cols, leaf_ids, top)
    owner = columns // leaf_dev
    others = (owner ^ row_index) & 1
    chips = size_rows // 2
    blocks = ((owner // 2 - row_index // 2) & (chips - 1)) * leaf_dev + columns % leaf_dev

    col = lax.axis_index("col").reshape(1).astype(jnp.int32)
    parts = partial_sketch(col, samples.T, in_hbm(sketch_matrix), size_cols)
    sk = sum_parts(lax.all_to_all(parts, "col", 0, 0), leaf_dev)
    mine, theirs = ring_gather(sk, size_rows)

    sums = products(slots, blocks, others, front_blocks, mine, theirs, size_cols)
    z = lax.all_to_all(sums, "col", 0, 0)
    parts = size_cols // leaf_dev
    col_index = lax.axis_index("col")
    place = jnp.stack([col_index // parts, col_index % parts]).astype(jnp.int32)
    basis, *groups = leaf_level(place, pick, z, parts)
    basis = lax.all_gather(basis, "col").reshape(leaf_dev * leaf_size, rank_size)
    for bit in range(leaf_dev.bit_length() - 1):
        stride = (parts << bit).bit_length() - 1
        side = (jnp.right_shift(col_index, stride) & 1).reshape(1).astype(jnp.int32)
        groups = climb(side, groups, "col", stride)
    bit = 0
    while len(groups) > 1:
        side = (jnp.right_shift(row_index, bit) & 1).reshape(1).astype(jnp.int32)
        groups = climb(side, groups, "row", bit)
        bit += 1
    first = groups[0][0]
    side = jnp.stack(
        [jnp.right_shift(row_index, bit) & 1, row_index % (size_rows // 2)]
    ).astype(jnp.int32)
    top_rows, basis = top_level(
        side, first, partner_2(first, "row", bit), 4 * rank_size // size_rows, in_hbm(basis)
    )
    return basis, top_rows


def solution(mesh):
    placed = (P("row", None, None, None), P("row", None), P("row", "col"), P())
    return jax.shard_map(
        shards,
        mesh=mesh,
        in_specs=placed,
        out_specs=(P("row", None), P("row", None)),
        check_vma=False,
    )
```

```python
import math

import jax
import jax.numpy as jnp
from jax import lax
from jax.experimental import pallas as pl
from jax.experimental.pallas import tpu as pltpu
from jax.sharding import PartitionSpec as P

F32 = jnp.float32
BF16 = jnp.bfloat16


NN = (((1,), (0,)), ((), ()))
NT = (((1,), (1,)), ((), ()))


def split(x):
    high = x.astype(BF16)
    return high, (x - high.astype(F32)).astype(BF16)


def product(a, b, dims):
    a_high, a_low = split(a)
    b_high, b_low = split(b)

    def dot(x, y):
        return lax.dot_general(x, y, dims, preferred_element_type=F32)

    return dot(a_high, b_high) + (dot(a_high, b_low) + dot(a_low, b_high))


def mm(a, b):
    return product(a, b, NN)


def mm_t(a, b):
    return product(a, b, NT)


def dot_t(a, b):
    return lax.dot_general(a, b, (((1,), (1,)), ((), ())), preferred_element_type=F32)


def factor64(blocks, width, paired, far):
    shape = blocks[0].shape
    sub = lax.broadcasted_iota(jnp.int32, shape, 1)
    rows = list(blocks)
    out = [None] * 8
    ahead = None
    for start in range(0, 64, width):
        own = start // 8
        below = list(range((start + width) // 8, 8))

        def spread(q):
            return [
                jnp.broadcast_to(rows[q][:, :, 64 + start + k : 65 + start + k], shape)
                for k in range(width)
            ]

        mine = ahead if ahead is not None else spread(own)
        ahead = None
        col = {q: list(mine) if q == own else spread(q) for q in below}
        late = [q for q in below if far and q > own + 2]
        near = [q for q in below if q not in late]
        a = [[None] * width for _ in range(width)]
        r = []
        for k in range(width):
            at = (start + k) % 8
            r.append(jnp.broadcast_to(rows[own][:, at : at + 1, :], shape))
            for i in range(k, width):
                at = (start + i) % 8
                a[i][k] = jnp.broadcast_to(mine[k][:, at : at + 1, :], shape)
        low = {q: [None] * width for q in near}
        step = own + 1
        if paired and step in near:
            ahead = [
                jnp.broadcast_to(rows[step][:, :, 72 + start + k : 73 + start + k], shape)
                for k in range(8)
            ]
        mult = [[None] * width for _ in range(width)]
        inv = [None] * width
        scaled = [None] * width
        if paired:
            pairs = []
            for j in range(0, width, 2):
                p, s, t = a[j][j], a[j + 1][j], a[j + 1][j + 1]
                root = lax.rsqrt(p * t - s * s)
                inv_det = root * root
                p_inv, s_inv, t_inv = t * inv_det, -(s * inv_det), p * inv_det
                m, n = {}, {}
                for k in range(j + 2, width):
                    m[k] = (t * a[k][j] - s * a[k][j + 1]) * inv_det
                    n[k] = (p * a[k][j + 1] - s * a[k][j]) * inv_det
                for k in range(j + 2, width):
                    for i in range(k, width):
                        a[i][k] = a[i][k] - (m[k] * a[i][j] + n[k] * a[i][j + 1])
                    r[k] = r[k] - (m[k] * r[j] + n[k] * r[j + 1])
                for q in near:
                    c, d = col[q][j], col[q][j + 1]
                    low[q][j] = c * p_inv + d * s_inv
                    low[q][j + 1] = c * s_inv + d * t_inv
                    for k in range(j + 2, width):
                        col[q][k] = col[q][k] - (m[k] * c + n[k] * d)
                    if q == step:
                        for k in range(8):
                            c_k = jnp.broadcast_to(c[:, k : k + 1, :], shape)
                            d_k = jnp.broadcast_to(d[:, k : k + 1, :], shape)
                            ahead[k] = ahead[k] - (low[q][j] * c_k + low[q][j + 1] * d_k)
                pairs.append((p_inv, s_inv, t_inv, m, n))
                first = lax.rsqrt(p)
                scaled[j] = r[j] * first
                scaled[j + 1] = (r[j + 1] - (s * (first * first)) * r[j]) * ((p * first) * root)
        else:
            for j in range(width):
                root = lax.rsqrt(a[j][j])
                inv[j] = root * root
                for k in range(j + 1, width):
                    mult[j][k] = a[k][j] * inv[j]
                for k in range(j + 1, width):
                    for i in range(k, width):
                        a[i][k] = a[i][k] - mult[j][k] * a[i][j]
                    r[k] = r[k] - mult[j][k] * r[j]
                for q in near:
                    low[q][j] = col[q][j] * inv[j]
                    for k in range(j + 1, width):
                        col[q][k] = col[q][k] - mult[j][k] * col[q][j]
                scaled[j] = r[j] * root
        for j in range(width):
            at = (start + j) % 8
            out[own] = scaled[j] if at == 0 else jnp.where(sub == at, scaled[j], out[own])
        solved = [None] * width
        if late and paired:
            for j in reversed(range(0, width, 2)):
                p_inv, s_inv, t_inv, m, n = pairs[j // 2]
                x = r[j] * p_inv + r[j + 1] * s_inv
                y = r[j] * s_inv + r[j + 1] * t_inv
                for k in range(j + 2, width):
                    x = x - m[k] * solved[k]
                    y = y - n[k] * solved[k]
                solved[j], solved[j + 1] = x, y
        elif late:
            for j in reversed(range(width)):
                value = r[j] * inv[j]
                for k in range(j + 1, width):
                    value = value - mult[j][k] * solved[k]
                solved[j] = value
        for q in below:
            if q in late:
                terms = [col[q][j] * solved[j] for j in range(width)]
            else:
                terms = [low[q][j] * r[j] for j in range(width)]
            while len(terms) > 1:
                terms = [terms[i] + terms[i + 1] for i in range(0, len(terms), 2)]
            rows[q] = rows[q] - terms[0]
    return out


FORMS = {1: (8, True, True), 2: (8, False, False), 4: (4, False, True)}


def inverse64(wide):
    lane = lax.broadcasted_iota(jnp.int32, (64, 128), 1)
    row = lax.broadcasted_iota(jnp.int32, (64, 128), 0)
    eye = (lane == row).astype(F32)
    full = [jnp.where(lane >= 64, w, eye) for w in wide]
    form = FORMS.get(len(wide), (4, False, True))
    out = factor64([jnp.stack([f[8 * i : 8 * i + 8] for f in full]) for i in range(8)], *form)
    return [jnp.concatenate([o[b] for o in out], axis=0) for b in range(len(wide))]


def inverse128(blocks):
    n = range(len(blocks))
    lane = lax.broadcasted_iota(jnp.int32, (64, 128), 1)
    row = lax.broadcasted_iota(jnp.int32, (64, 128), 0)
    first = inverse64([pltpu.roll(b[:64], 64, 1) for b in blocks])
    first = [jnp.where(lane < 64, f, 0.0) for f in first]
    right = [mm(first[i][:, :64], blocks[i][:64]) for i in n]
    left = [mm_t(blocks[i][64:, :64], first[i][:, :64]) for i in n]
    schur = [blocks[i][64:] - mm(left[i], right[i]) for i in n]
    mixed = [mm(left[i], first[i]) for i in n]
    second = inverse64(schur)
    eye = (lane == row + 64).astype(F32)
    low = [mm(second[i][:, :64], jnp.where(lane < 64, -mixed[i], eye)) for i in n]
    return [jnp.concatenate([first[i], low[i]], axis=0) for i in n]


def cholqr_t(z_ts, gram_ref, between=None):
    n = range(len(z_ts))
    half = z_ts[0].shape[0] // 2
    for i in n:
        gram_ref[i] = dot_t(z_ts[i], z_ts[i])
    first = inverse128([gram_ref[i, 0:half, 0:half] for i in n])
    right = [mm(first[i], gram_ref[i, 0:half, half:]) for i in n]
    left = [mm_t(gram_ref[i, half:, 0:half], first[i]) for i in n]
    schur = [gram_ref[i, half:, half:] - mm(left[i], right[i]) for i in n]
    top = []
    for i in n:
        high, low = split(first[i])
        z_1 = z_ts[i][:half]
        top.append(
            jnp.dot(high, z_1, preferred_element_type=F32)
            + jnp.dot(low, z_1, preferred_element_type=F32)
        )
    below = [z_ts[i][half:].astype(F32) - mm(left[i], top[i]) for i in n]
    if between is not None:
        between()
    second = inverse128(schur)
    scale = math.sqrt(z_ts[0].shape[1])
    return [jnp.concatenate([top[i], mm(second[i], below[i])], axis=0) * scale for i in n]


VMEM = pl.BlockSpec(memory_space=pltpu.MemorySpace.VMEM)
SMEM = pl.BlockSpec(memory_space=pltpu.MemorySpace.SMEM)
HBM = pl.BlockSpec(memory_space=pltpu.MemorySpace.HBM)
PARAMS = pltpu.CompilerParams(vmem_limit_bytes=48 << 20)


def in_hbm(x):
    return pltpu.with_memory_space_constraint(x, pltpu.MemorySpace.HBM)


def partial_kernel(col_ref, x_t_ref, w_ref, out_ref):
    part = lax.dot_general(
        w_ref[...], x_t_ref[...], (((0,), (0,)), ((), ())), preferred_element_type=F32
    )
    out_ref[...] = part.astype(BF16).reshape(out_ref.shape)


def partial_sketch(col, x_t, w, size_cols):
    depth, rows = x_t.shape
    rank = w.shape[1]
    shape = (size_cols, rank // size_cols, rows)
    return pl.pallas_call(
        partial_kernel,
        out_shape=jax.ShapeDtypeStruct(shape, BF16),
        grid_spec=pltpu.PrefetchScalarGridSpec(
            num_scalar_prefetch=1,
            grid=(1,),
            in_specs=[
                pl.BlockSpec((depth, rows), lambda i, col: (0, 0)),
                pl.BlockSpec((depth, rank), lambda i, col: (col[0], 0)),
            ],
            out_specs=pl.BlockSpec(shape, lambda i, col: (0, 0, 0)),
        ),
        compiler_params=PARAMS,
    )(col, x_t, w)


def sum_kernel(parts_ref, out_ref):
    leaves, _, size = out_ref.shape
    for m in range(leaves):
        at = slice(m * size, (m + 1) * size)
        total = parts_ref[0, :, at].astype(F32)
        for s in range(1, parts_ref.shape[0]):
            total = total + parts_ref[s, :, at].astype(F32)
        out_ref[m] = total.astype(BF16)


def sum_parts(parts, leaves):
    _, cols, rows = parts.shape
    return pl.pallas_call(
        sum_kernel,
        out_shape=jax.ShapeDtypeStruct((leaves, cols, rows // leaves), BF16),
        in_specs=[VMEM],
        out_specs=VMEM,
        compiler_params=PARAMS,
    )(parts)


def products_kernel(
    slot_ref, block_ref, other_ref, front_ref, mine_ref, theirs_ref, out_ref, held_ref, sems
):
    leaves, steps = slot_ref.shape
    copies_in = [
        [
            pltpu.make_async_copy(
                front_ref.at[m, slot_ref[m, s]], held_ref.at[m, s], sems.at[m, s]
            )
            for s in range(steps)
        ]
        for m in range(leaves)
    ]
    for m in range(leaves):
        for s in range(steps):
            copies_in[m][s].start()
    cols = mine_ref.shape[1]
    copies = out_ref.shape[0] // leaves
    for m in range(leaves):
        total = None
        for s in range(steps):
            block = block_ref[m, s]
            sk = jnp.where(other_ref[m, s] == 0, mine_ref[block], theirs_ref[block])
            wide = jnp.concatenate([sk] * (steps - s) + [jnp.zeros_like(sk)] * s, axis=0)
            copies_in[m][s].wait()
            part = dot_t(wide, held_ref[m, s])
            total = part if total is None else total + part
        sums = total.astype(BF16).reshape(steps, cols, total.shape[1])
        for d in range(copies):
            out_ref[m * copies + d] = sums


def products(slots, blocks, others, front, mine, theirs, peers):
    leaves, _, size, _ = front.shape
    steps = slots.shape[1]
    cols = mine.shape[1]
    return pl.pallas_call(
        products_kernel,
        out_shape=jax.ShapeDtypeStruct((peers, steps, cols, size), BF16),
        in_specs=[SMEM, SMEM, SMEM, HBM, VMEM, VMEM],
        out_specs=VMEM,
        scratch_shapes=[
            pltpu.VMEM((leaves, steps, size, size), BF16),
            pltpu.SemaphoreType.DMA((leaves, steps)),
        ],
        compiler_params=PARAMS,
    )(slots, blocks, others, front, mine, theirs)


def rows_of(q_t, start, count):
    shape = (count, q_t.shape[1])
    lane = lax.broadcasted_iota(jnp.int32, shape, 1)
    chosen = lane == lax.broadcasted_iota(jnp.int32, shape, 0) + start
    return dot_t(chosen.astype(F32).astype(BF16), q_t).astype(BF16)


def leaf_kernel(place_ref, pick_ref, z_ref, part_ref, first_ref, second_ref, rest_ref, gram_ref):
    sources, _, cols, size = z_ref.shape
    rank = sources * cols
    leaf = place_ref[0]
    q_t = cholqr_t([z_ref[:, 0].reshape(rank, size)], gram_ref)[0]
    basis_t = q_t.astype(BF16)
    scale = 1.0 / math.sqrt(size)
    for level in range(pick_ref.shape[1]):
        proj = move(z_ref[:, pick_ref[leaf, level]].reshape(rank, size), basis_t, scale)
        if level == 0:
            first_ref[0] = proj
        elif level == 1:
            second_ref[0] = proj
        else:
            rest_ref[level - 2] = proj
    part_ref[...] = rows_of(basis_t, place_ref[1] * part_ref.shape[0], part_ref.shape[0])


def leaf_level(place, pick, z, parts):
    sources, _, cols, size = z.shape
    rank = sources * cols
    return pl.pallas_call(
        leaf_kernel,
        out_shape=(
            jax.ShapeDtypeStruct((size // parts, rank), BF16),
            jax.ShapeDtypeStruct((1, rank, rank), BF16),
            jax.ShapeDtypeStruct((1, rank, rank), BF16),
            jax.ShapeDtypeStruct((pick.shape[1] - 2, rank, rank), BF16),
        ),
        in_specs=[SMEM, SMEM, VMEM],
        out_specs=(VMEM, VMEM, VMEM, VMEM),
        scratch_shapes=[pltpu.VMEM((1, rank, rank), F32)],
        compiler_params=PARAMS,
    )(place, pick, z)


def move(stacked, transfer, scale):
    return (dot_t(stacked, transfer) * scale).astype(BF16)


def pair_t(side_ref, own, partner):
    is_left = side_ref[0] == 0
    left = jnp.where(is_left, own, partner)
    right = jnp.where(is_left, partner, own)
    return jnp.concatenate([left, right], axis=1)


def transfer_kernel(side_ref, own_ref, partner_ref, out_ref, gram_ref):
    z_t = pair_t(side_ref, own_ref[...], partner_ref[...])
    out_ref[...] = cholqr_t([z_t], gram_ref)[0].astype(BF16)


def transfer(side, own, partner):
    rank = own.shape[0]
    return pl.pallas_call(
        transfer_kernel,
        out_shape=jax.ShapeDtypeStruct((rank, 2 * rank), BF16),
        in_specs=[SMEM, VMEM, VMEM],
        out_specs=VMEM,
        scratch_shapes=[pltpu.VMEM((1, rank, rank), F32)],
        compiler_params=PARAMS,
    )(side, own, partner)


def moves_kernel(side_ref, e_t_ref, own_ref, partner_ref, out_ref):
    levels, rank, _ = own_ref.shape
    scale = 1.0 / math.sqrt(2 * rank)
    for level in range(levels):
        z_t = pair_t(side_ref, own_ref[level], partner_ref[level])
        out_ref[level] = move(z_t, e_t_ref[...], scale)


def moves(side, e_t, own, partner):
    return pl.pallas_call(
        moves_kernel,
        out_shape=jax.ShapeDtypeStruct(own.shape, BF16),
        in_specs=[SMEM, VMEM, VMEM, VMEM],
        out_specs=VMEM,
        compiler_params=PARAMS,
    )(side, e_t, own, partner)


def climb(side, groups, axis, mask):
    first, *groups = lax.optimization_barrier((partner_2(groups[0], axis, mask), *groups))
    theirs = [first] + [partner_2(group, axis, mask) for group in groups[1:]]
    e_t = transfer(side, groups[0][0], theirs[0][0])
    moved = [moves(side, e_t, own, other) for own, other in zip(groups[1:], theirs[1:])]
    if len(moved) == 1 or moved[1].shape[0] == 1:
        return moved
    return [moved[0], moved[1][:1], moved[1][1:]]


def top_level_kernel(
    side_ref, own_ref, partner_ref, basis_ref, out_ref, basis_out_ref, gram_ref, held_ref, sems
):
    copy_in = pltpu.make_async_copy(basis_ref, held_ref, sems.at[0])
    copy_out = pltpu.make_async_copy(held_ref, basis_out_ref, sems.at[1])

    def pass_on():
        copy_in.wait()
        copy_out.start()

    copy_in.start()
    rows = out_ref.shape[0]
    z_t = pair_t(side_ref, own_ref[...], partner_ref[...])
    e_t = cholqr_t([z_t], gram_ref, pass_on)[0]
    out_ref[...] = rows_of(e_t.astype(BF16), side_ref[1] * rows, rows)
    copy_out.wait()


def top_level(side, own, partner, rows, basis):
    rank = own.shape[0]
    return pl.pallas_call(
        top_level_kernel,
        out_shape=(
            jax.ShapeDtypeStruct((rows, rank), BF16),
            jax.ShapeDtypeStruct(basis.shape, BF16),
        ),
        in_specs=[SMEM, VMEM, VMEM, HBM],
        out_specs=(VMEM, HBM),
        scratch_shapes=[
            pltpu.VMEM((1, rank, rank), F32),
            pltpu.VMEM(basis.shape, BF16),
            pltpu.SemaphoreType.DMA((2,)),
        ],
        compiler_params=PARAMS,
    )(side, own, partner, basis)


def plan(block_cols, leaf_ids, top_level):
    level_ids = jnp.arange(top_level, dtype=jnp.int32)
    near = block_cols[:, 2:]
    outside = (
        jnp.right_shift(leaf_ids[:, None, None], level_ids)
        != jnp.right_shift(near[:, :, None], level_ids)
    )
    drop = jnp.sum(outside.astype(jnp.int32), axis=2)
    count = near.shape[1]
    slot_ids = jnp.arange(count, dtype=jnp.int32)
    before = (drop[:, None, :] > drop[:, :, None]) | (
        (drop[:, None, :] == drop[:, :, None]) & (slot_ids[None, None, :] < slot_ids[None, :, None])
    )
    rank = jnp.sum(before.astype(jnp.int32), axis=2)
    chosen = (rank[:, None, :] == slot_ids[None, :, None]).astype(jnp.int32)
    one = jnp.ones_like(near[:, :1])
    slots = jnp.concatenate([one, jnp.sum(chosen * (slot_ids + 2), axis=2)], axis=1)
    blocks = jnp.concatenate([block_cols[:, 1:2], jnp.sum(chosen * near[:, None, :], axis=2)], axis=1)
    pick = jnp.sum((drop[:, None, :] <= level_ids[None, 1:, None]).astype(jnp.int32), axis=2)
    return slots, blocks, pick


def ring_gather(piece, size_rows):
    chips = size_rows // 2

    def ahead(value, distance):
        pairs = [
            (2 * z + k, 2 * ((z - distance) % chips) + k) for z in range(chips) for k in range(2)
        ]
        return lax.ppermute(value, "row", pairs)

    count = piece.shape[0]
    at_4, at_2, at_6 = lax.optimization_barrier(
        (ahead(piece, 4), ahead(piece, 2), ahead(piece, -2))
    )
    both = jnp.concatenate([piece, at_4], axis=0)
    at_1_5, at_7_3 = ahead(both, 1), ahead(both, -1)
    mine = jnp.concatenate(
        [piece, at_1_5[:count], at_2, at_7_3[count:], at_4, at_1_5[count:], at_6, at_7_3[:count]],
        axis=0,
    )
    return mine, partner_2(mine, "row", 1)


def partner_2(value, axis, mask):
    pairs = [(source, source ^ mask) for source in range(lax.axis_size(axis))]
    return lax.ppermute(value, axis, pairs)


def shards(front_blocks, block_cols, samples, sketch_matrix):
    leaf_dev, _, leaf_size, _ = front_blocks.shape
    rank_size = sketch_matrix.shape[1]
    size_rows, size_cols = lax.axis_size("row"), lax.axis_size("col")
    row_index = lax.axis_index("row")
    top = (leaf_dev * size_rows).bit_length() - 1
    leaf_ids = row_index * leaf_dev + jnp.arange(leaf_dev, dtype=jnp.int32)
    slots, columns, pick = plan(block_cols, leaf_ids, top)
    owner = columns // leaf_dev
    others = (owner ^ row_index) & 1
    chips = size_rows // 2
    blocks = ((owner // 2 - row_index // 2) & (chips - 1)) * leaf_dev + columns % leaf_dev

    col = lax.axis_index("col").reshape(1).astype(jnp.int32)
    parts = partial_sketch(col, samples.T, in_hbm(sketch_matrix), size_cols)
    sk = sum_parts(lax.all_to_all(parts, "col", 0, 0), leaf_dev)
    mine, theirs = ring_gather(sk, size_rows)

    sums = products(slots, blocks, others, front_blocks, mine, theirs, size_cols)
    z = lax.all_to_all(sums, "col", 0, 0)
    parts = size_cols // leaf_dev
    col_index = lax.axis_index("col")
    place = jnp.stack([col_index // parts, col_index % parts]).astype(jnp.int32)
    basis, *groups = leaf_level(place, pick, z, parts)
    basis = lax.all_gather(basis, "col").reshape(leaf_dev * leaf_size, rank_size)
    for bit in range(leaf_dev.bit_length() - 1):
        stride = (parts << bit).bit_length() - 1
        side = (jnp.right_shift(col_index, stride) & 1).reshape(1).astype(jnp.int32)
        groups = climb(side, groups, "col", parts * ((2 << bit) - 1))
    bit = 0
    while len(groups) > 1:
        side = (jnp.right_shift(row_index, bit) & 1).reshape(1).astype(jnp.int32)
        groups = climb(side, groups, "row", 1 << bit)
        bit += 1
    first = groups[0][0]
    side = jnp.stack(
        [jnp.right_shift(row_index, bit) & 1, row_index % (size_rows // 2)]
    ).astype(jnp.int32)
    top_rows, basis = top_level(
        side, first, partner_2(first, "row", 1 << bit), 4 * rank_size // size_rows, in_hbm(basis)
    )
    return basis, top_rows


def solution(mesh):
    placed = (P("row", None, None, None), P("row", None), P("row", "col"), P())
    return jax.shard_map(
        shards,
        mesh=mesh,
        in_specs=placed,
        out_specs=(P("row", None), P("row", None)),
        check_vma=False,
    )
```

```python
import math

import jax
import jax.numpy as jnp
from jax import lax
from jax.experimental import pallas as pl
from jax.experimental.pallas import tpu as pltpu
from jax.sharding import PartitionSpec as P

F32 = jnp.float32
BF16 = jnp.bfloat16


NN = (((1,), (0,)), ((), ()))
NT = (((1,), (1,)), ((), ()))


def split(x):
    high = x.astype(BF16)
    return high, (x - high.astype(F32)).astype(BF16)


def product(a, b, dims):
    a_high, a_low = split(a)
    b_high, b_low = split(b)

    def dot(x, y):
        return lax.dot_general(x, y, dims, preferred_element_type=F32)

    return dot(a_high, b_high) + (dot(a_high, b_low) + dot(a_low, b_high))


def mm(a, b):
    return product(a, b, NN)


def mm_t(a, b):
    return product(a, b, NT)


def dot_t(a, b):
    return lax.dot_general(a, b, (((1,), (1,)), ((), ())), preferred_element_type=F32)


def factor64(blocks, width, paired, far):
    shape = blocks[0].shape
    sub = lax.broadcasted_iota(jnp.int32, shape, 1)
    rows = list(blocks)
    out = [None] * 8
    ahead = None
    for start in range(0, 64, width):
        own = start // 8
        below = list(range((start + width) // 8, 8))

        def spread(q):
            return [
                jnp.broadcast_to(rows[q][:, :, 64 + start + k : 65 + start + k], shape)
                for k in range(width)
            ]

        mine = ahead if ahead is not None else spread(own)
        ahead = None
        col = {q: list(mine) if q == own else spread(q) for q in below}
        late = [q for q in below if far and q > own + 2]
        near = [q for q in below if q not in late]
        a = [[None] * width for _ in range(width)]
        r = []
        for k in range(width):
            at = (start + k) % 8
            r.append(jnp.broadcast_to(rows[own][:, at : at + 1, :], shape))
            for i in range(k, width):
                at = (start + i) % 8
                a[i][k] = jnp.broadcast_to(mine[k][:, at : at + 1, :], shape)
        low = {q: [None] * width for q in near}
        step = own + 1
        if paired and step in near:
            ahead = [
                jnp.broadcast_to(rows[step][:, :, 72 + start + k : 73 + start + k], shape)
                for k in range(8)
            ]
        mult = [[None] * width for _ in range(width)]
        inv = [None] * width
        scaled = [None] * width
        if paired:
            pairs = []
            for j in range(0, width, 2):
                p, s, t = a[j][j], a[j + 1][j], a[j + 1][j + 1]
                root = lax.rsqrt(p * t - s * s)
                inv_det = root * root
                p_inv, s_inv, t_inv = t * inv_det, -(s * inv_det), p * inv_det
                m, n = {}, {}
                for k in range(j + 2, width):
                    m[k] = (t * a[k][j] - s * a[k][j + 1]) * inv_det
                    n[k] = (p * a[k][j + 1] - s * a[k][j]) * inv_det
                for k in range(j + 2, width):
                    for i in range(k, width):
                        a[i][k] = a[i][k] - (m[k] * a[i][j] + n[k] * a[i][j + 1])
                    r[k] = r[k] - (m[k] * r[j] + n[k] * r[j + 1])
                for q in near:
                    c, d = col[q][j], col[q][j + 1]
                    low[q][j] = c * p_inv + d * s_inv
                    low[q][j + 1] = c * s_inv + d * t_inv
                    for k in range(j + 2, width):
                        col[q][k] = col[q][k] - (m[k] * c + n[k] * d)
                    if q == step:
                        for k in range(8):
                            c_k = jnp.broadcast_to(c[:, k : k + 1, :], shape)
                            d_k = jnp.broadcast_to(d[:, k : k + 1, :], shape)
                            ahead[k] = ahead[k] - (low[q][j] * c_k + low[q][j + 1] * d_k)
                pairs.append((p_inv, s_inv, t_inv, m, n))
                first = lax.rsqrt(p)
                scaled[j] = r[j] * first
                scaled[j + 1] = (r[j + 1] - (s * (first * first)) * r[j]) * ((p * first) * root)
        else:
            for j in range(width):
                root = lax.rsqrt(a[j][j])
                inv[j] = root * root
                for k in range(j + 1, width):
                    mult[j][k] = a[k][j] * inv[j]
                for k in range(j + 1, width):
                    for i in range(k, width):
                        a[i][k] = a[i][k] - mult[j][k] * a[i][j]
                    r[k] = r[k] - mult[j][k] * r[j]
                for q in near:
                    low[q][j] = col[q][j] * inv[j]
                    for k in range(j + 1, width):
                        col[q][k] = col[q][k] - mult[j][k] * col[q][j]
                scaled[j] = r[j] * root
        for j in range(width):
            at = (start + j) % 8
            out[own] = scaled[j] if at == 0 else jnp.where(sub == at, scaled[j], out[own])
        solved = [None] * width
        if late and paired:
            for j in reversed(range(0, width, 2)):
                p_inv, s_inv, t_inv, m, n = pairs[j // 2]
                x = r[j] * p_inv + r[j + 1] * s_inv
                y = r[j] * s_inv + r[j + 1] * t_inv
                for k in range(j + 2, width):
                    x = x - m[k] * solved[k]
                    y = y - n[k] * solved[k]
                solved[j], solved[j + 1] = x, y
        elif late:
            for j in reversed(range(width)):
                value = r[j] * inv[j]
                for k in range(j + 1, width):
                    value = value - mult[j][k] * solved[k]
                solved[j] = value
        for q in below:
            if q in late:
                terms = [col[q][j] * solved[j] for j in range(width)]
            else:
                terms = [low[q][j] * r[j] for j in range(width)]
            while len(terms) > 1:
                terms = [terms[i] + terms[i + 1] for i in range(0, len(terms), 2)]
            rows[q] = rows[q] - terms[0]
    return out


FORMS = {1: (8, True, True), 2: (8, False, False), 4: (4, False, True)}


def inverse64(wide):
    lane = lax.broadcasted_iota(jnp.int32, (64, 128), 1)
    row = lax.broadcasted_iota(jnp.int32, (64, 128), 0)
    eye = (lane == row).astype(F32)
    full = [jnp.where(lane >= 64, w, eye) for w in wide]
    form = FORMS.get(len(wide), (4, False, True))
    out = factor64([jnp.stack([f[8 * i : 8 * i + 8] for f in full]) for i in range(8)], *form)
    return [jnp.concatenate([o[b] for o in out], axis=0) for b in range(len(wide))]


def inverse128(blocks):
    n = range(len(blocks))
    lane = lax.broadcasted_iota(jnp.int32, (64, 128), 1)
    row = lax.broadcasted_iota(jnp.int32, (64, 128), 0)
    first = inverse64([pltpu.roll(b[:64], 64, 1) for b in blocks])
    first = [jnp.where(lane < 64, f, 0.0) for f in first]
    right = [mm(first[i][:, :64], blocks[i][:64]) for i in n]
    left = [mm_t(blocks[i][64:, :64], first[i][:, :64]) for i in n]
    schur = [blocks[i][64:] - mm(left[i], right[i]) for i in n]
    mixed = [mm(left[i], first[i]) for i in n]
    second = inverse64(schur)
    eye = (lane == row + 64).astype(F32)
    low = [mm(second[i][:, :64], jnp.where(lane < 64, -mixed[i], eye)) for i in n]
    return [jnp.concatenate([first[i], low[i]], axis=0) for i in n]


def cholqr_t(z_ts, gram_ref, between=None):
    n = range(len(z_ts))
    half = z_ts[0].shape[0] // 2
    for i in n:
        gram_ref[i] = dot_t(z_ts[i], z_ts[i])
    first = inverse128([gram_ref[i, 0:half, 0:half] for i in n])
    right = [mm(first[i], gram_ref[i, 0:half, half:]) for i in n]
    left = [mm_t(gram_ref[i, half:, 0:half], first[i]) for i in n]
    schur = [gram_ref[i, half:, half:] - mm(left[i], right[i]) for i in n]
    top = []
    for i in n:
        high, low = split(first[i])
        z_1 = z_ts[i][:half]
        top.append(
            jnp.dot(high, z_1, preferred_element_type=F32)
            + jnp.dot(low, z_1, preferred_element_type=F32)
        )
    below = [z_ts[i][half:].astype(F32) - mm(left[i], top[i]) for i in n]
    if between is not None:
        between()
    second = inverse128(schur)
    scale = math.sqrt(z_ts[0].shape[1])
    return [jnp.concatenate([top[i], mm(second[i], below[i])], axis=0) * scale for i in n]


VMEM = pl.BlockSpec(memory_space=pltpu.MemorySpace.VMEM)
SMEM = pl.BlockSpec(memory_space=pltpu.MemorySpace.SMEM)
HBM = pl.BlockSpec(memory_space=pltpu.MemorySpace.HBM)
PARAMS = pltpu.CompilerParams(vmem_limit_bytes=48 << 20)


def in_hbm(x):
    return pltpu.with_memory_space_constraint(x, pltpu.MemorySpace.HBM)


def partial_kernel(col_ref, x_t_ref, w_ref, out_ref):
    part = lax.dot_general(
        w_ref[...], x_t_ref[...], (((0,), (0,)), ((), ())), preferred_element_type=F32
    )
    out_ref[...] = part.astype(BF16).reshape(out_ref.shape)


def partial_sketch(col, x_t, w, size_cols):
    depth, rows = x_t.shape
    rank = w.shape[1]
    shape = (size_cols, rank // size_cols, rows)
    return pl.pallas_call(
        partial_kernel,
        out_shape=jax.ShapeDtypeStruct(shape, BF16),
        grid_spec=pltpu.PrefetchScalarGridSpec(
            num_scalar_prefetch=1,
            grid=(1,),
            in_specs=[
                pl.BlockSpec((depth, rows), lambda i, col: (0, 0)),
                pl.BlockSpec((depth, rank), lambda i, col: (col[0], 0)),
            ],
            out_specs=pl.BlockSpec(shape, lambda i, col: (0, 0, 0)),
        ),
        compiler_params=PARAMS,
    )(col, x_t, w)


def sum_kernel(parts_ref, out_ref):
    leaves, _, size = out_ref.shape
    for m in range(leaves):
        at = slice(m * size, (m + 1) * size)
        total = parts_ref[0, :, at].astype(F32)
        for s in range(1, parts_ref.shape[0]):
            total = total + parts_ref[s, :, at].astype(F32)
        out_ref[m] = total.astype(BF16)


def sum_parts(parts, leaves):
    _, cols, rows = parts.shape
    return pl.pallas_call(
        sum_kernel,
        out_shape=jax.ShapeDtypeStruct((leaves, cols, rows // leaves), BF16),
        in_specs=[VMEM],
        out_specs=VMEM,
        compiler_params=PARAMS,
    )(parts)


def products_kernel(
    slot_ref, block_ref, other_ref, front_ref, mine_ref, theirs_ref, out_ref, held_ref, sems
):
    leaves, steps = slot_ref.shape
    copies_in = [
        [
            pltpu.make_async_copy(
                front_ref.at[m, slot_ref[m, s]], held_ref.at[m, s], sems.at[m, s]
            )
            for s in range(steps)
        ]
        for m in range(leaves)
    ]
    for m in range(leaves):
        for s in range(steps):
            copies_in[m][s].start()
    cols = mine_ref.shape[1]
    copies = out_ref.shape[0] // leaves
    for m in range(leaves):
        total = None
        for s in range(steps):
            block = block_ref[m, s]
            sk = jnp.where(other_ref[m, s] == 0, mine_ref[block], theirs_ref[block])
            wide = jnp.concatenate([sk] * (steps - s) + [jnp.zeros_like(sk)] * s, axis=0)
            copies_in[m][s].wait()
            part = dot_t(wide, held_ref[m, s])
            total = part if total is None else total + part
        sums = total.astype(BF16).reshape(steps, cols, total.shape[1])
        for d in range(copies):
            out_ref[m * copies + d] = sums


def products(slots, blocks, others, front, mine, theirs, peers):
    leaves, _, size, _ = front.shape
    steps = slots.shape[1]
    cols = mine.shape[1]
    return pl.pallas_call(
        products_kernel,
        out_shape=jax.ShapeDtypeStruct((peers, steps, cols, size), BF16),
        in_specs=[SMEM, SMEM, SMEM, HBM, VMEM, VMEM],
        out_specs=VMEM,
        scratch_shapes=[
            pltpu.VMEM((leaves, steps, size, size), BF16),
            pltpu.SemaphoreType.DMA((leaves, steps)),
        ],
        compiler_params=PARAMS,
    )(slots, blocks, others, front, mine, theirs)


def rows_of(q_t, start, count):
    shape = (count, q_t.shape[1])
    lane = lax.broadcasted_iota(jnp.int32, shape, 1)
    chosen = lane == lax.broadcasted_iota(jnp.int32, shape, 0) + start
    return dot_t(chosen.astype(F32).astype(BF16), q_t).astype(BF16)


def leaf_kernel(place_ref, pick_ref, z_ref, part_ref, first_ref, second_ref, rest_ref, gram_ref):
    sources, _, cols, size = z_ref.shape
    rank = sources * cols
    leaf = place_ref[0]
    q_t = cholqr_t([z_ref[:, 0].reshape(rank, size)], gram_ref)[0]
    basis_t = q_t.astype(BF16)
    scale = 1.0 / math.sqrt(size)
    for level in range(pick_ref.shape[1]):
        proj = move(z_ref[:, pick_ref[leaf, level]].reshape(rank, size), basis_t, scale)
        if level == 0:
            first_ref[0] = proj
        elif level == 1:
            second_ref[0] = proj
        else:
            rest_ref[level - 2] = proj
    part_ref[...] = rows_of(basis_t, place_ref[1] * part_ref.shape[0], part_ref.shape[0])


def leaf_level(place, pick, z, parts):
    sources, _, cols, size = z.shape
    rank = sources * cols
    return pl.pallas_call(
        leaf_kernel,
        out_shape=(
            jax.ShapeDtypeStruct((size // parts, rank), BF16),
            jax.ShapeDtypeStruct((1, rank, rank), BF16),
            jax.ShapeDtypeStruct((1, rank, rank), BF16),
            jax.ShapeDtypeStruct((pick.shape[1] - 2, rank, rank), BF16),
        ),
        in_specs=[SMEM, SMEM, VMEM],
        out_specs=(VMEM, VMEM, VMEM, VMEM),
        scratch_shapes=[pltpu.VMEM((1, rank, rank), F32)],
        compiler_params=PARAMS,
    )(place, pick, z)


def move(stacked, transfer, scale):
    return (dot_t(stacked, transfer) * scale).astype(BF16)


def pair_t(side_ref, own, partner):
    is_left = side_ref[0] == 0
    left = jnp.where(is_left, own, partner)
    right = jnp.where(is_left, partner, own)
    return jnp.concatenate([left, right], axis=1)


def transfer_kernel(side_ref, own_ref, partner_ref, out_ref, gram_ref):
    z_t = pair_t(side_ref, own_ref[...], partner_ref[...])
    out_ref[...] = cholqr_t([z_t], gram_ref)[0].astype(BF16)


def transfer(side, own, partner):
    rank = own.shape[0]
    return pl.pallas_call(
        transfer_kernel,
        out_shape=jax.ShapeDtypeStruct((rank, 2 * rank), BF16),
        in_specs=[SMEM, VMEM, VMEM],
        out_specs=VMEM,
        scratch_shapes=[pltpu.VMEM((1, rank, rank), F32)],
        compiler_params=PARAMS,
    )(side, own, partner)


def moves_kernel(side_ref, e_t_ref, own_ref, partner_ref, out_ref):
    levels, rank, _ = own_ref.shape
    scale = 1.0 / math.sqrt(2 * rank)
    for level in range(levels):
        z_t = pair_t(side_ref, own_ref[level], partner_ref[level])
        out_ref[level] = move(z_t, e_t_ref[...], scale)


def moves(side, e_t, own, partner):
    return pl.pallas_call(
        moves_kernel,
        out_shape=jax.ShapeDtypeStruct(own.shape, BF16),
        in_specs=[SMEM, VMEM, VMEM, VMEM],
        out_specs=VMEM,
        compiler_params=PARAMS,
    )(side, e_t, own, partner)


def climb(side, groups, axis, mask):
    first, *groups = lax.optimization_barrier((partner_2(groups[0], axis, mask), *groups))
    theirs = [first] + [partner_2(group, axis, mask) for group in groups[1:]]
    e_t = transfer(side, groups[0][0], theirs[0][0])
    moved = [moves(side, e_t, own, other) for own, other in zip(groups[1:], theirs[1:])]
    if len(moved) == 1 or moved[1].shape[0] == 1:
        return moved
    return [moved[0], moved[1][:1], moved[1][1:]]


def top_level_kernel(
    side_ref, own_ref, partner_ref, basis_ref, out_ref, basis_out_ref, gram_ref, held_ref, sems
):
    copy_in = pltpu.make_async_copy(basis_ref, held_ref, sems.at[0])
    copy_out = pltpu.make_async_copy(held_ref, basis_out_ref, sems.at[1])

    def pass_on():
        copy_in.wait()
        copy_out.start()

    copy_in.start()
    rows = out_ref.shape[0]
    z_t = pair_t(side_ref, own_ref[...], partner_ref[...])
    e_t = cholqr_t([z_t], gram_ref, pass_on)[0]
    out_ref[...] = rows_of(e_t.astype(BF16), side_ref[1] * rows, rows)
    copy_out.wait()


def top_level(side, own, partner, rows, basis):
    rank = own.shape[0]
    return pl.pallas_call(
        top_level_kernel,
        out_shape=(
            jax.ShapeDtypeStruct((rows, rank), BF16),
            jax.ShapeDtypeStruct(basis.shape, BF16),
        ),
        in_specs=[SMEM, VMEM, VMEM, HBM],
        out_specs=(VMEM, HBM),
        scratch_shapes=[
            pltpu.VMEM((1, rank, rank), F32),
            pltpu.VMEM(basis.shape, BF16),
            pltpu.SemaphoreType.DMA((2,)),
        ],
        compiler_params=PARAMS,
    )(side, own, partner, basis)


def plan(block_cols, leaf_ids, top_level):
    level_ids = jnp.arange(top_level, dtype=jnp.int32)
    near = block_cols[:, 2:]
    outside = (
        jnp.right_shift(leaf_ids[:, None, None], level_ids)
        != jnp.right_shift(near[:, :, None], level_ids)
    )
    drop = jnp.sum(outside.astype(jnp.int32), axis=2)
    count = near.shape[1]
    slot_ids = jnp.arange(count, dtype=jnp.int32)
    before = (drop[:, None, :] > drop[:, :, None]) | (
        (drop[:, None, :] == drop[:, :, None]) & (slot_ids[None, None, :] < slot_ids[None, :, None])
    )
    rank = jnp.sum(before.astype(jnp.int32), axis=2)
    chosen = (rank[:, None, :] == slot_ids[None, :, None]).astype(jnp.int32)
    one = jnp.ones_like(near[:, :1])
    slots = jnp.concatenate([one, jnp.sum(chosen * (slot_ids + 2), axis=2)], axis=1)
    blocks = jnp.concatenate([block_cols[:, 1:2], jnp.sum(chosen * near[:, None, :], axis=2)], axis=1)
    pick = jnp.sum((drop[:, None, :] <= level_ids[None, 1:, None]).astype(jnp.int32), axis=2)
    return slots, blocks, pick


def ring_gather(piece, size_rows):
    chips = size_rows // 2

    def ahead(value, distance):
        pairs = [
            (2 * z + k, 2 * ((z - distance) % chips) + k) for z in range(chips) for k in range(2)
        ]
        return lax.ppermute(value, "row", pairs)

    count = piece.shape[0]
    at_1, at_7, at_4 = lax.optimization_barrier(
        (ahead(piece, 1), ahead(piece, -1), ahead(piece, 4))
    )
    at_2_3 = ahead(jnp.concatenate([piece, at_1], axis=0), 2)
    at_6_5 = ahead(jnp.concatenate([piece, at_7], axis=0), -2)
    mine = jnp.concatenate(
        [piece, at_1, at_2_3, at_4, at_6_5[count:], at_6_5[:count], at_7], axis=0
    )
    return mine, partner_2(mine, "row", 1)


def partner_2(value, axis, mask):
    pairs = [(source, source ^ mask) for source in range(lax.axis_size(axis))]
    return lax.ppermute(value, axis, pairs)


def shards(front_blocks, block_cols, samples, sketch_matrix):
    leaf_dev, _, leaf_size, _ = front_blocks.shape
    rank_size = sketch_matrix.shape[1]
    size_rows, size_cols = lax.axis_size("row"), lax.axis_size("col")
    row_index = lax.axis_index("row")
    top = (leaf_dev * size_rows).bit_length() - 1
    leaf_ids = row_index * leaf_dev + jnp.arange(leaf_dev, dtype=jnp.int32)
    slots, columns, pick = plan(block_cols, leaf_ids, top)
    owner = columns // leaf_dev
    others = (owner ^ row_index) & 1
    chips = size_rows // 2
    blocks = ((owner // 2 - row_index // 2) & (chips - 1)) * leaf_dev + columns % leaf_dev

    col = lax.axis_index("col").reshape(1).astype(jnp.int32)
    parts = partial_sketch(col, samples.T, in_hbm(sketch_matrix), size_cols)
    sk = sum_parts(lax.all_to_all(parts, "col", 0, 0), leaf_dev)
    mine, theirs = ring_gather(sk, size_rows)

    sums = products(slots, blocks, others, front_blocks, mine, theirs, size_cols)
    z = lax.all_to_all(sums, "col", 0, 0)
    parts = size_cols // leaf_dev
    col_index = lax.axis_index("col")
    place = jnp.stack([col_index // parts, col_index % parts]).astype(jnp.int32)
    basis, *groups = leaf_level(place, pick, z, parts)
    basis = lax.all_gather(basis, "col").reshape(leaf_dev * leaf_size, rank_size)
    for bit in range(leaf_dev.bit_length() - 1):
        stride = (parts << bit).bit_length() - 1
        side = (jnp.right_shift(col_index, stride) & 1).reshape(1).astype(jnp.int32)
        groups = climb(side, groups, "col", parts * ((2 << bit) - 1))
    bit = 0
    while len(groups) > 1:
        side = (jnp.right_shift(row_index, bit) & 1).reshape(1).astype(jnp.int32)
        groups = climb(side, groups, "row", 1 << bit)
        bit += 1
    first = groups[0][0]
    side = jnp.stack(
        [jnp.right_shift(row_index, bit) & 1, row_index % (size_rows // 2)]
    ).astype(jnp.int32)
    top_rows, basis = top_level(
        side, first, partner_2(first, "row", 1 << bit), 4 * rank_size // size_rows, in_hbm(basis)
    )
    return basis, top_rows


def solution(mesh):
    placed = (P("row", None, None, None), P("row", None), P("row", "col"), P())
    return jax.shard_map(
        shards,
        mesh=mesh,
        in_specs=placed,
        out_specs=(P("row", None), P("row", None)),
        check_vma=False,
    )
```
